32 devices in a mesh: seq: 8 (over z, y), tp: 4 (over x, core).
Axes of the slice: x: 2, y: 2, z: 4, core: 2. Of those that a mesh axis runs over, the one named last changes fastest.
Arguments:
- tokens: bfloat16 [8, 2048, 1024], P(None, 'seq'), may hold values from -6 to 6
- seg_ids: int32 [8, 2048], replicated, may hold values from 0 to 3, never falling along the last dimension, each value on 1 to 1024 neighbouring positions
- routed_index: int32 [8, 256], replicated, may hold values from 0 to 2047, as said below
- gain_attn: bfloat16 [1024], replicated, may hold values from 0.099609375 to 1.8984375
- w_qkv: bfloat16 [1024, 3, 1024], P(None, None, 'tp'), may hold values from -0.1875 to 0.1875
- w_out: bfloat16 [1024, 1024], P('tp'), may hold values from -0.375 to 0.375
- gain_mlp: bfloat16 [1024], replicated, may hold values from 0.099609375 to 1.8984375
- w_up: bfloat16 [1024, 4096], P(None, 'tp'), may hold values from -0.1875 to 0.1875
- w_down: bfloat16 [4096, 1024], P('tp'), may hold values from -0.09375 to 0.09375
- w_router: bfloat16 [1024], replicated, may hold values from -0.1875 to 0.1875
- out_grad: bfloat16 [8, 2048, 1024], P(None, 'seq'), may hold values from -6 to 6
Outputs:
- block_out: bfloat16 [8, 2048, 1024], P(None, 'seq')
- grad_tokens: float32 [8, 2048, 1024], P(None, 'seq')
- grad_gain_attn: float32 [1024], P('seq')
- grad_qkv: float32 [1024, 3, 1024], P('seq', None, 'tp')
- grad_out: float32 [1024, 1024], P('tp', 'seq')
- grad_gain_mlp: float32 [1024], P('seq')
- grad_up: float32 [1024, 4096], P('seq', 'tp')
- grad_down: float32 [4096, 1024], P('tp', 'seq')
- grad_router: float32 [1024], P('seq')
The draws below stay inside these ranges and needn't reach their ends.
Inputs may be any that keep to these rules, and one draw needn't show every extreme that they name: `routed_index`: each row lists the 256 routed positions of one sequence, all different, in rising order. Cutting a sequence into blocks of 256 positions, the position of rank r lies in block r // 32 or in the block before it; some block holds 64 routed positions.
All inputs are finite; a program needn't handle non-finite values.
Results may differ from the reference program's by a relative error of at most 0.018.
Values may be sent and summed in bfloat16 or wider, within the bound.
No kernel may reach another device: no remote copies, remote signals or barrier semaphores. Data moves between devices by JAX's collectives and lax.ppermute only.
A program may use at most 384 MiB of HBM per device.

```python
import math
import jax
import jax.numpy as jnp
import numpy as np
from jax import lax

D = 1024
HEADS = 16
HEAD_DIM = 64
FF = 4096
SEQS = 8
GROUP = 256
SEQ_LEN = 2048
ROUTED = 256
SHARE = 32


def draw_routed_index(key, part):
    dev_count = SEQ_LEN // GROUP
    key_moved, key_picked = jax.random.split(jax.random.fold_in(key, 7))
    moved = jax.random.randint(key_moved, (SEQS, dev_count), 0, SHARE + 1)
    at_last = jnp.arange(dev_count) == dev_count - 1
    moved = jnp.where(at_last[None, :], 0, moved)
    moved = moved.at[0, 0].set(SHARE)
    before = jnp.concatenate([jnp.zeros((SEQS, 1), jnp.int32), moved[:, :-1]], axis=1)
    counts = SHARE + moved - before
    noise = jax.random.randint(key_picked, (SEQS, dev_count, GROUP), 0, 65536)
    scores = noise * GROUP + jnp.arange(GROUP, dtype=jnp.int32)[None, None, :]
    order = jnp.argsort(jnp.argsort(scores, axis=-1), axis=-1)
    chosen = (order < counts[:, :, None]).reshape(SEQS, SEQ_LEN)
    ranks = jnp.cumsum(chosen.astype(jnp.int32), axis=1) - 1
    target = jnp.where(chosen, ranks, ROUTED)
    places = jnp.broadcast_to(jnp.arange(SEQ_LEN, dtype=jnp.int32)[None, :], (SEQS, SEQ_LEN))
    seq_rows = jnp.broadcast_to(jnp.arange(SEQS, dtype=jnp.int32)[:, None], (SEQS, SEQ_LEN))
    result = jnp.zeros((SEQS, ROUTED), jnp.int32).at[seq_rows, target].set(places, mode='drop')
    return result


def with_spikes(values, stream_key, source, target, parts, factor):
    owner, partner = [(jnp.arange(values.shape[position]) // (values.shape[position] // parts)).reshape([-1 if axis == position else 1 for axis in range(values.ndim)]) for position in (source, target)]
    chosen = jax.random.permutation(stream_key, parts)[partner]
    strong = (owner == chosen) | (owner == (partner + parts // 2) % parts)
    return jnp.where(strong, factor * values, values)


def block_scale(rng, shape, pieces, low, largest):
    def one(position, blocks):
        heights = jax.random.uniform(jax.random.fold_in(jax.random.fold_in(rng, 6), position), (blocks,), jnp.float32, low / len(pieces), largest / len(pieces))
        return jnp.repeat(jnp.exp(heights), shape[position] // blocks).reshape((-1,) + (1,) * (len(shape) - position - 1))

    loudness = one(*pieces[0])
    for cut in pieces[1:]:
        loudness = loudness * one(*cut)
    return loudness


def split_up(amount, total, limit, slope):
    weights = [(1 << 20) // math.isqrt(grade ** slope) + 1 for grade in range(2, amount + 1)]
    spare, holding = total - limit - (amount - 1), [1] * (amount - 1)
    while spare > 0:
        free = [i for i in range(amount - 1) if holding[i] < limit]
        pool, left = sum([weights[i] for i in free]), spare
        for i in free:
            addition = min(limit - holding[i], max(1, left * weights[i] // pool), spare)
            holding[i] = holding[i] + addition
            spare = spare - addition
    return np.array([limit] + holding)


def uneven_parts(stream_key, number_of, total, most, lean):
    if number_of == 2:
        one = jax.random.randint(stream_key, (), max(1, total - most), min(most, total - 1) + 1)
        return jnp.stack([one, total - one])
    tallies = jnp.asarray(split_up(number_of, total, most, lean), jnp.int32)
    twos = (number_of - 1) // 2
    donor, taker = tallies[1:1 + 2 * twos:2], tallies[2:2 + 2 * twos:2]
    slack = jnp.minimum(donor - 1, most - taker)
    shifted = jax.random.randint(jax.random.fold_in(stream_key, 1), (twos,), 0, 1 << 20) % (slack + 1)
    tallies = tallies.at[1:1 + 2 * twos:2].set(donor - shifted).at[2:2 + 2 * twos:2].set(taker + shifted)
    return tallies[jax.random.permutation(jax.random.fold_in(stream_key, 2), number_of)]


def normal_values(own_key, shape, spread, limit, shards=(), held_as=jnp.bfloat16):
    drawn = jax.random.normal(own_key, shape, jnp.float32) * spread
    if len(shards) > 0:
        drawn = block_scale(own_key, shape, shards, -0.22, 0.18) * drawn
    return jnp.clip(drawn, min=-limit, max=limit).astype(held_as)


def heavy_noise(own_key, shape, deviation, bound, shards, heavy, kind=jnp.bfloat16):
    values = deviation * jax.random.normal(own_key, shape, jnp.float32)
    if shards:
        values = values * block_scale(own_key, shape, shards, -0.22, 0.18)
    return jnp.clip(with_spikes(values, jax.random.fold_in(own_key, 3), *heavy), -bound, bound).astype(kind)


def setup_inputs(seed: int = 0) -> dict:
    keys = jax.random.split(jax.random.key(seed), 12)
    return {
        "tokens": heavy_noise(keys[0], (SEQS, SEQ_LEN, D), 1.0, 6.0, ((1, 8),), (1, 2, 8, 2.0)),
        "seg_ids": jax.vmap(lambda own: jnp.searchsorted(jnp.cumsum(uneven_parts(own, 4, SEQ_LEN, SEQ_LEN // 2, 0)), jnp.arange(SEQ_LEN), side="right"))(jax.random.split(keys[1], SEQS)).reshape((SEQS, SEQ_LEN)).astype(jnp.int32),
        "routed_index": draw_routed_index(jax.random.fold_in(keys[11], 71), 0),
        "gain_attn": jnp.clip(1.0 + 0.18 * jax.random.normal(keys[3], (D,), jnp.float32), 0.099609375, 1.8984375).astype(jnp.bfloat16),
        "w_qkv": normal_values(keys[4], (D, 3, HEADS * HEAD_DIM), D ** -0.5, 0.1875, ((2, 4),)),
        "w_out": normal_values(keys[5], (HEADS * HEAD_DIM, D), (HEADS * HEAD_DIM // 4) ** -0.5, 0.375, ((0, 4),)),
        "gain_mlp": jnp.clip(1.0 + 0.18 * jax.random.normal(keys[6], (D,), jnp.float32), 0.099609375, 1.8984375).astype(jnp.bfloat16),
        "w_up": normal_values(keys[7], (D, FF), D ** -0.5, 0.1875, ((1, 4),)),
        "w_down": normal_values(keys[8], (FF, D), FF ** -0.5, 0.09375, ((0, 4),)),
        "w_router": normal_values(keys[9], (D,), D ** -0.5, 0.1875),
        "out_grad": heavy_noise(keys[10], (SEQS, SEQ_LEN, D), 1.0, 6.0, ((1, 8),), (1, 2, 8, 2.0)),
    }


@jax.custom_vjp
def low(v):
    return lax.optimization_barrier(v.astype(jnp.bfloat16)).astype(jnp.float32)

@jax.custom_vjp
def low_back(v):
    return v

def low_keep(v):
    return (low(v), None)

def low_pass(kept, grad):
    return (grad,)

def back_keep(v):
    return (v, None)

def back_low(kept, grad):
    return (low(grad),)
low.defvjp(low_keep, low_pass)
low_back.defvjp(back_keep, back_low)
precise = lax.Precision.HIGHEST

def normed(values, gain):
    factor = lax.rsqrt(lax.optimization_barrier(jnp.mean(values * values, axis=-1, keepdims=True)) + 1e-05)
    return values * factor * gain

def block_sequence(tokens_row, seg_row, index_row, gain_attn, w_qkv, w_out, gain_mlp, w_up, w_down, w_router):
    routed = low_back(tokens_row[index_row])
    row_count = index_row.shape[0]
    gating = jax.nn.sigmoid(jnp.dot(routed, w_router, precision=precise))
    attn_input = low(normed(routed, gain_attn))
    qkv_rows = low_back(low(jnp.einsum('rd,dch->rch', attn_input, w_qkv, precision=precise)))
    head_count = w_qkv.shape[2] // HEAD_DIM
    queries = qkv_rows[:, 0].reshape(row_count, head_count, HEAD_DIM)
    all_keys = qkv_rows[:, 1].reshape(row_count, head_count, HEAD_DIM)
    all_values = qkv_rows[:, 2].reshape(row_count, head_count, HEAD_DIM)
    raw_scores = low_back(jnp.einsum('qhe,khe->hqk', queries, all_keys, precision=precise))
    seg_routed = seg_row[index_row]
    ranks = jnp.arange(row_count, dtype=jnp.int32)
    allowed = jnp.logical_and(ranks[None, :] <= ranks[:, None], seg_routed[None, :] == seg_routed[:, None])
    logits = jnp.where(allowed[None], raw_scores * HEAD_DIM ** (-0.5), -1e+30)
    probs_low = low(jax.nn.softmax(logits, axis=-1))
    mixed = jnp.einsum('hqk,khe->qhe', probs_low, all_values, precision=precise).reshape(row_count, -1)
    mixed = low_back(low(mixed))
    attn_out = low_back(jnp.dot(mixed, w_out, precision=precise))
    residual = routed + attn_out
    mlp_input = low(normed(residual, gain_mlp))
    pre_act = low_back(jnp.dot(mlp_input, w_up, precision=precise))
    hidden = low(jax.nn.gelu(pre_act, approximate=True))
    mlp_out = low_back(jnp.dot(hidden, w_down, precision=precise))
    update = low(gating[:, None] * (attn_out + mlp_out))
    return tokens_row.at[index_row].add(update)

def reference(tokens, seg_ids, routed_index, gain_attn, w_qkv, w_out, gain_mlp, w_up, w_down, w_router, out_grad):
    params = tuple((weight.astype(jnp.float32) for weight in (gain_attn, w_qkv, w_out, gain_mlp, w_up, w_down, w_router)))

    def one_sequence(totals, inputs):
        tokens_row, seg_row, index_row, grad_row = inputs

        def forward(row_values, *weights):
            return block_sequence(row_values, seg_row, index_row, *weights)
        output, pullback = jax.vjp(forward, tokens_row.astype(jnp.float32), *params)
        grads = pullback(grad_row.astype(jnp.float32))
        totals = tuple((total + grad for total, grad in zip(totals, grads[1:])))
        return (totals, (output.astype(jnp.bfloat16), grads[0]))
    zeros = tuple((jnp.zeros(weight.shape, jnp.float32) for weight in params))
    totals, (outputs, token_grads) = lax.scan(one_sequence, zeros, (tokens, seg_ids, routed_index, out_grad))
    return (outputs, token_grads, totals[0], totals[1], totals[2], totals[3], totals[4], totals[5], totals[6])
```

```python
import jax
import jax.numpy as jnp
from jax import lax
from jax.sharding import PartitionSpec as P

HEAD_DIM = 64


precise = lax.Precision.HIGHEST


def normed(values, gain):
    factor = lax.rsqrt(jnp.mean(values * values, axis=-1, keepdims=True) + 1e-05)
    return values * factor * gain


def gelu_tanh(values):
    return jax.nn.gelu(values, approximate=True)


def match_table(positions, usable, anchor, extent):
    offsets = jnp.arange(extent, dtype=jnp.int32)
    hits = (positions - anchor)[:, :, None] == offsets[None, None, :]
    return jnp.logical_and(hits, usable[:, :, None]).astype(jnp.bfloat16)


def compact(table, source):
    return jnp.einsum("sqc,scd->sqd", table, source, preferred_element_type=jnp.float32)


def spread(table, routed_rows):
    return jnp.einsum("sqc,sqd->scd", table, routed_rows, preferred_element_type=jnp.float32)


def on_device_split(
    tokens,
    seg_ids,
    routed_index,
    gain_attn,
    w_qkv,
    w_out,
    gain_mlp,
    w_up,
    w_down,
    w_router,
    out_grad,
):
    seq_count, group_len, model_width = tokens.shape
    routed_len = routed_index.shape[1]
    dev_count = lax.axis_size("seq")
    dev_index = lax.axis_index("seq")
    per_dev = routed_len // dev_count
    group_base = dev_index * group_len
    seg_routed = jnp.take_along_axis(seg_ids, routed_index, axis=1)
    capacity = 2 * per_dev
    slot_ids = jnp.arange(capacity, dtype=jnp.int32)
    first_rank = jnp.sum((routed_index < group_base).astype(jnp.int32), axis=1)
    group_count = (
        jnp.sum((routed_index < group_base + group_len).astype(jnp.int32), axis=1) - first_rank
    )
    query_rank = first_rank[:, None] + slot_ids[None, :]
    query_valid = slot_ids[None, :] < group_count[:, None]
    clipped = jnp.minimum(query_rank, routed_len - 1)
    query_pos = jnp.take_along_axis(routed_index, clipped, axis=1)
    own_table = match_table(query_pos, query_valid, group_base, group_len)
    routed_rows = compact(own_table, tokens).astype(jnp.bfloat16)
    routed_grads = compact(own_table, out_grad).astype(jnp.bfloat16)
    query_seg = jnp.take_along_axis(seg_routed, clipped, axis=1)
    bounds = jnp.arange(dev_count, dtype=jnp.int32) * group_len
    firsts = jnp.sum((routed_index[:, :, None] < bounds[None, None, :]).astype(jnp.int32), axis=1)
    next_firsts = jnp.concatenate(
        [firsts[:, 1:], jnp.full((seq_count, 1), routed_len, jnp.int32)], axis=1
    )
    key_rank = (firsts[:, :, None] + slot_ids[None, None, :]).reshape(seq_count, -1)
    key_valid = (slot_ids[None, None, :] < (next_firsts - firsts)[:, :, None]).reshape(
        seq_count, -1
    )
    key_seg = jnp.take_along_axis(seg_routed, jnp.minimum(key_rank, routed_len - 1), axis=1)
    allowed = jnp.logical_and(
        key_rank[:, None, :] <= query_rank[:, :, None], key_seg[:, None, :] == query_seg[:, :, None]
    )
    allowed = jnp.logical_and(allowed, key_valid[:, None, :])[:, None]
    rows_float = routed_rows.astype(jnp.float32)
    gain_first = gain_attn.astype(jnp.float32)
    gain_second = gain_mlp.astype(jnp.float32)
    router_score = jnp.einsum(
        "sqd,d->sq", routed_rows, w_router, preferred_element_type=jnp.float32
    )
    gating = jax.nn.sigmoid(router_score)
    attn_input = normed(rows_float, gain_first).astype(jnp.bfloat16)
    qkv_rows = jnp.einsum(
        "sqd,dch->sqch", attn_input, w_qkv, preferred_element_type=jnp.float32
    ).astype(jnp.bfloat16)
    query_count = qkv_rows.shape[1]
    head_count = qkv_rows.shape[3] // HEAD_DIM
    query_flat = qkv_rows[:, :, 0]
    queries = query_flat.reshape(seq_count, query_count, head_count, HEAD_DIM)
    key_pair = (qkv_rows[:, :, 1], qkv_rows[:, :, 2])
    all_keys = lax.all_gather(key_pair[0], "seq", axis=1, tiled=True)
    all_values = lax.all_gather(key_pair[1], "seq", axis=1, tiled=True)
    key_count = all_keys.shape[1]
    all_keys = all_keys.reshape(seq_count, key_count, head_count, HEAD_DIM)
    all_values = all_values.reshape(seq_count, key_count, head_count, HEAD_DIM)
    scaling = HEAD_DIM ** (-0.5)

    def masked_logits():
        raw_scores = jnp.einsum(
            "sqhe,skhe->shqk", queries, all_keys, preferred_element_type=jnp.float32
        )
        return jnp.where(allowed, raw_scores * scaling, -1e30)

    logits = masked_logits()
    row_peak = jnp.max(logits, axis=-1, keepdims=True)
    powered = jnp.exp(logits - row_peak)
    row_total = jnp.sum(powered, axis=-1, keepdims=True)
    log_total = row_peak + jnp.log(row_total)
    probs_low = (powered / row_total).astype(jnp.bfloat16)
    mixed = jnp.einsum("shqk,skhe->sqhe", probs_low, all_values, preferred_element_type=jnp.float32)
    mixed = mixed.reshape(seq_count, query_count, -1).astype(jnp.bfloat16)
    attn_out = lax.psum(
        jnp.einsum("sqh,hd->sqd", mixed, w_out, preferred_element_type=jnp.float32).astype(
            jnp.bfloat16
        ),
        "tp",
    ).astype(jnp.float32)
    residual = rows_float + attn_out
    mlp_input = normed(residual, gain_second).astype(jnp.bfloat16)
    pre_act = jnp.einsum("sqd,df->sqf", mlp_input, w_up, preferred_element_type=jnp.float32)
    hidden = gelu_tanh(pre_act).astype(jnp.bfloat16)
    mlp_out = lax.psum(
        jnp.einsum("sqf,fd->sqd", hidden, w_down, preferred_element_type=jnp.float32).astype(
            jnp.bfloat16
        ),
        "tp",
    ).astype(jnp.float32)
    branch = attn_out + mlp_out
    update_rows = (gating[:, :, None] * branch).astype(jnp.bfloat16)
    block_out = (tokens.astype(jnp.float32) + spread(own_table, update_rows)).astype(jnp.bfloat16)
    grad_rows = routed_grads.astype(jnp.float32)
    scaled_grad = gating[:, :, None] * grad_rows
    grad_score = jnp.sum(grad_rows * branch, axis=-1) * gating * (1.0 - gating)
    grad_mlp = scaled_grad.astype(jnp.bfloat16)
    grad_down = jnp.einsum("sqf,sqd->fd", hidden, grad_mlp, preferred_element_type=jnp.float32)
    grad_hidden = jnp.einsum("sqd,fd->sqf", grad_mlp, w_down, preferred_element_type=jnp.float32)
    gelu_pull = jax.vjp(gelu_tanh, pre_act)[1]
    grad_pre = gelu_pull(grad_hidden)[0].astype(jnp.bfloat16)
    grad_up = jnp.einsum("sqd,sqf->df", mlp_input, grad_pre, preferred_element_type=jnp.float32)
    grad_mlp_input = lax.psum(
        jnp.einsum("sqf,df->sqd", grad_pre, w_up, preferred_element_type=jnp.float32).astype(
            jnp.bfloat16
        ),
        "tp",
    ).astype(jnp.float32)
    second_pull = jax.vjp(normed, residual, gain_second)[1]
    grad_residual, grad_gain_mlp = second_pull(grad_mlp_input)
    grad_attn = (grad_residual + scaled_grad).astype(jnp.bfloat16)
    grad_out = jnp.einsum("sqh,sqd->hd", mixed, grad_attn, preferred_element_type=jnp.float32)
    grad_mixed_flat = jnp.einsum(
        "sqd,hd->sqh", grad_attn, w_out, preferred_element_type=jnp.float32
    ).astype(jnp.bfloat16)
    grad_mixed = grad_mixed_flat.reshape(seq_count, query_count, head_count, HEAD_DIM)
    probs_again = jnp.where(allowed, jnp.exp(masked_logits() - log_total), 0.0)
    grad_probs = jnp.einsum(
        "sqhe,skhe->shqk", grad_mixed, all_values, preferred_element_type=jnp.float32
    )
    inner_sum = jnp.sum(probs_again * grad_probs, axis=-1, keepdims=True)
    grad_raw = (probs_again * (grad_probs - inner_sum) * scaling).astype(jnp.bfloat16)
    grad_query = jnp.einsum(
        "shqk,skhe->sqhe", grad_raw, all_keys, preferred_element_type=jnp.float32
    )
    grad_query = grad_query.reshape(seq_count, query_count, -1).astype(jnp.bfloat16)
    probs_again_low = probs_again.astype(jnp.bfloat16)
    key_part = jnp.einsum(
        "shqk,sqhe->skhe", grad_raw, queries, preferred_element_type=jnp.float32
    ).reshape(seq_count, key_count, -1)
    value_part = jnp.einsum(
        "shqk,sqhe->skhe", probs_again_low, grad_mixed, preferred_element_type=jnp.float32
    ).reshape(seq_count, key_count, -1)
    key_pair = (key_part, value_part)
    grad_keys = lax.psum_scatter(key_pair[0], "seq", scatter_dimension=1, tiled=True)
    grad_values = lax.psum_scatter(key_pair[1], "seq", scatter_dimension=1, tiled=True)
    grad_qkv_rows = jnp.stack(
        [grad_query, grad_keys.astype(jnp.bfloat16), grad_values.astype(jnp.bfloat16)], axis=2
    )
    grad_qkv = jnp.einsum(
        "sqd,sqch->dch", attn_input, grad_qkv_rows, preferred_element_type=jnp.float32
    )
    grad_attn_input = lax.psum(
        jnp.einsum(
            "sqch,dch->sqd", grad_qkv_rows, w_qkv, preferred_element_type=jnp.float32
        ).astype(jnp.bfloat16),
        "tp",
    ).astype(jnp.float32)
    first_pull = jax.vjp(normed, rows_float, gain_first)[1]
    grad_norm, grad_gain_attn = first_pull(grad_attn_input)
    grad_router = jnp.einsum("sq,sqd->d", grad_score, rows_float, precision=precise)
    grad_routed_in = (
        grad_residual + grad_norm + grad_score[:, :, None] * w_router.astype(jnp.float32)
    ).astype(jnp.bfloat16)
    grad_tokens = out_grad.astype(jnp.float32) + spread(own_table, grad_routed_in)
    reduced = (
        lax.psum_scatter(grad_gain_attn, "seq", scatter_dimension=0, tiled=True),
        lax.psum_scatter(grad_qkv, "seq", scatter_dimension=0, tiled=True),
        lax.psum_scatter(grad_out, "seq", scatter_dimension=1, tiled=True),
        lax.psum_scatter(grad_gain_mlp, "seq", scatter_dimension=0, tiled=True),
        lax.psum_scatter(grad_up, "seq", scatter_dimension=0, tiled=True),
        lax.psum_scatter(grad_down, "seq", scatter_dimension=1, tiled=True),
        lax.psum_scatter(grad_router, "seq", scatter_dimension=0, tiled=True),
    )
    return (block_out, grad_tokens) + tuple(reduced)


def ring_order(size):
    return list(range(0, size, 2)) + list(range(size - 1, 0, -2))


def ring_permute(values, order, step):
    size = len(order)
    pairs = [(order[i], order[(i + step) % size]) for i in range(size)]
    return lax.ppermute(values, "seq", pairs)


def ring_scatter(parts, direction):
    size = parts.shape[0]
    order = ring_order(size)
    place = [order.index(i) for i in range(size)]
    table = [
        [order[(place[i] - direction * (1 + k)) % size] for k in range(size)] for i in range(size)
    ]
    mine = jnp.asarray(table, dtype=jnp.int32)[lax.axis_index("seq")]
    total = lax.dynamic_index_in_dim(parts, mine[0], 0, False)
    for k in range(1, size):
        moved = ring_permute(total, order, direction)
        own = lax.dynamic_index_in_dim(parts, mine[k], 0, False)
        total = moved.astype(jnp.float32) + own.astype(jnp.float32)
        if k < size - 1:
            total = total.astype(jnp.bfloat16)
    return total


def tp_permute(values, mask):
    size = lax.axis_size("tp")
    return lax.ppermute(values, "tp", [(i, i ^ mask) for i in range(size)])


def pick_half(values, which):
    width = values.shape[-1] // 2
    return jnp.where(which == 0, values[..., :width], values[..., width:])


def join_halves(own, other, which):
    return jnp.where(
        which == 0,
        jnp.concatenate([own, other], axis=-1),
        jnp.concatenate([other, own], axis=-1),
    )


def tp_sum(partial, which):
    narrow = partial.astype(jnp.bfloat16)
    moved = tp_permute(pick_half(narrow, 1 - which), 1)
    half = pick_half(partial, which) + moved.astype(jnp.float32)
    half = half.astype(jnp.bfloat16)
    moved = tp_permute(half, 2)
    half = (half.astype(jnp.float32) + moved.astype(jnp.float32)).astype(jnp.bfloat16)
    return join_halves(half, tp_permute(half, 1), which).astype(jnp.float32)


def to_owners(rows, share):
    groups = rows.reshape(-1, share, rows.shape[-1])
    later = jnp.concatenate([groups[1:], jnp.zeros_like(groups[:1])], axis=0)
    return jnp.concatenate([groups, later], axis=1)


def from_owners(slots, share):
    later = jnp.concatenate([jnp.zeros_like(slots[:1, share:]), slots[:-1, share:]], axis=0)
    return (slots[:, :share] + later).reshape(-1, slots.shape[-1])


def on_device_whole(
    tokens,
    seg_ids,
    routed_index,
    gain_attn,
    w_qkv,
    w_out,
    gain_mlp,
    w_up,
    w_down,
    w_router,
    out_grad,
):
    f32, bf16 = jnp.float32, jnp.bfloat16
    seq_count, group_len, model_width = tokens.shape
    routed_len = routed_index.shape[1]
    dev_count = lax.axis_size("seq")
    dev_index = lax.axis_index("seq")
    core = lax.axis_index("tp") % 2
    share = routed_len // dev_count
    half_width = model_width // 2

    padded_index = jnp.concatenate(
        [routed_index, jnp.full((seq_count, share), -1, jnp.int32)], axis=1
    )
    slots = lax.dynamic_slice(padded_index, (0, dev_index * share), (seq_count, 2 * share))
    offsets = jnp.arange(group_len, dtype=jnp.int32)
    table = ((slots - dev_index * group_len)[:, :, None] == offsets).astype(bf16)

    index_row = lax.dynamic_index_in_dim(routed_index, dev_index, 0, False)
    seg_row = lax.dynamic_index_in_dim(seg_ids, dev_index, 0, False)
    seg_routed = sum(
        (index_row >= jnp.sum((seg_row < t).astype(jnp.int32))).astype(jnp.int32)
        for t in range(1, 4)
    )
    ranks = jnp.arange(routed_len, dtype=jnp.int32)
    allowed = jnp.logical_and(
        ranks[None, :] <= ranks[:, None], seg_routed[None, :] == seg_routed[:, None]
    )[None]

    def fetch(source):
        own = lax.dynamic_slice_in_dim(source, core * half_width, half_width, 2)
        return compact(table, own).astype(bf16)

    sent = jnp.concatenate([fetch(tokens), fetch(out_grad)], axis=-1)
    got = lax.all_to_all(sent, "seq", 0, 0, tiled=True)
    got = from_owners(got, share)
    other = tp_permute(got, 1)
    routed_rows = join_halves(got[:, :half_width], other[:, :half_width], core)
    routed_grads = join_halves(got[:, half_width:], other[:, half_width:], core)

    rows = routed_rows.astype(f32)
    grad_rows = routed_grads.astype(f32)
    gain_first = gain_attn.astype(f32)
    gain_second = gain_mlp.astype(f32)
    router = w_router.astype(f32)
    gating = jax.nn.sigmoid(jnp.sum(rows * router, axis=-1, keepdims=True))
    factor_first = lax.rsqrt(jnp.mean(rows * rows, axis=-1, keepdims=True) + 1e-05)
    attn_input = (rows * factor_first * gain_first).astype(bf16)
    weights = jnp.transpose(w_qkv, (1, 0, 2))
    qkv = jnp.einsum("rd,cdh->crh", attn_input, weights, preferred_element_type=f32).astype(bf16)
    head_count = qkv.shape[2] // HEAD_DIM
    scaling = HEAD_DIM ** (-0.5)

    def heads(values):
        return values.reshape(routed_len, head_count, HEAD_DIM)

    queries, keys, values = heads(qkv[0]), heads(qkv[1]), heads(qkv[2])
    raw = jnp.einsum("qhe,khe->hqk", queries, keys, preferred_element_type=f32)
    logits = jnp.where(allowed, raw * scaling, -1e30)
    powered = jnp.exp(logits - jnp.max(logits, axis=-1, keepdims=True))
    probs = powered / jnp.sum(powered, axis=-1, keepdims=True)
    probs_low = probs.astype(bf16)
    mixed = jnp.einsum("hqk,khe->qhe", probs_low, values, preferred_element_type=f32)
    mixed = mixed.reshape(routed_len, -1).astype(bf16)
    attn_out = tp_sum(jnp.dot(mixed, w_out, preferred_element_type=f32), core)

    residual = rows + attn_out
    factor_second = lax.rsqrt(jnp.mean(residual * residual, axis=-1, keepdims=True) + 1e-05)
    mlp_input = (residual * factor_second * gain_second).astype(bf16)
    scaled_grad = gating * grad_rows
    grad_mlp = scaled_grad.astype(bf16)
    pre_act = jnp.dot(mlp_input, w_up, preferred_element_type=f32)
    hidden, gelu_pull = jax.vjp(gelu_tanh, pre_act)
    hidden = hidden.astype(bf16)
    grad_hidden = lax.dot_general(
        grad_mlp, w_down, (((1,), (1,)), ((), ())), preferred_element_type=f32
    )
    grad_pre = gelu_pull(grad_hidden)[0].astype(bf16)
    grad_mlp_input = tp_sum(
        lax.dot_general(grad_pre, w_up, (((1,), (1,)), ((), ())), preferred_element_type=f32), core
    )
    mlp_out = tp_sum(jnp.dot(hidden, w_down, preferred_element_type=f32), core)

    def outer(left, right):
        product = lax.dot_general(
            left, right, (((0,), (0,)), ((), ())), preferred_element_type=f32
        )
        return product.astype(bf16).reshape(dev_count, -1, right.shape[1])

    grad_up = ring_scatter(outer(mlp_input, grad_pre), 1)
    grad_down = ring_scatter(outer(grad_mlp, hidden), -1).T

    weighted = grad_mlp_input * gain_second
    grad_residual = factor_second * weighted - residual * factor_second**3 * jnp.mean(
        residual * weighted, axis=-1, keepdims=True
    )
    grad_gain_mlp = jnp.sum(grad_mlp_input * residual * factor_second, axis=0)
    grad_attn = (grad_residual + scaled_grad).astype(bf16)
    grad_mixed = lax.dot_general(
        grad_attn, w_out, (((1,), (1,)), ((), ())), preferred_element_type=f32
    ).astype(bf16)
    grad_heads = heads(grad_mixed)
    grad_probs = jnp.einsum("qhe,khe->hqk", grad_heads, values, preferred_element_type=f32)
    inner_sum = jnp.sum(probs * grad_probs, axis=-1, keepdims=True)
    grad_raw = (probs * (grad_probs - inner_sum) * scaling).astype(bf16)

    def flat(products):
        return products.reshape(routed_len, -1).astype(bf16)

    grad_query = flat(jnp.einsum("hqk,khe->qhe", grad_raw, keys, preferred_element_type=f32))
    grad_key = flat(jnp.einsum("hqk,qhe->khe", grad_raw, queries, preferred_element_type=f32))
    grad_value = flat(jnp.einsum("hqk,qhe->khe", probs_low, grad_heads, preferred_element_type=f32))
    grad_parts = (grad_query, grad_key, grad_value)
    grad_attn_input = tp_sum(
        sum(
            lax.dot_general(
                grad_parts[c], weights[c], (((1,), (1,)), ((), ())), preferred_element_type=f32
            )
            for c in range(3)
        ),
        core,
    )
    forth = jnp.concatenate([outer(attn_input, grad_query), outer(attn_input, grad_key)], axis=-1)
    back = jnp.concatenate([outer(attn_input, grad_value), outer(grad_attn, mixed)], axis=-1)
    forth = ring_scatter(forth, 1)
    back = ring_scatter(back, -1)
    width = grad_query.shape[1]
    grad_qkv = jnp.stack([forth[:, :width], forth[:, width:], back[:, :width]], axis=1)
    grad_out = back[:, width:].T

    branch = attn_out + mlp_out
    update = (gating * branch).astype(bf16)
    grad_score = gating * (1.0 - gating) * jnp.sum(grad_rows * branch, axis=-1, keepdims=True)
    weighted = grad_attn_input * gain_first
    grad_norm = factor_first * weighted - rows * factor_first**3 * jnp.mean(
        rows * weighted, axis=-1, keepdims=True
    )
    grad_gain_attn = jnp.sum(grad_attn_input * rows * factor_first, axis=0)
    grad_router = jnp.sum(grad_score * rows, axis=0)
    grad_routed_in = (grad_residual + grad_norm + grad_score * router).astype(bf16)

    small = jnp.stack([grad_gain_attn, grad_gain_mlp, grad_router]).astype(bf16)
    small = small.reshape(3, dev_count, -1).transpose(1, 0, 2)
    small = jnp.pad(small, ((0, 0), (0, 13), (0, half_width - small.shape[2])))
    sent = to_owners(pick_half(update, core), share)
    got_update = lax.all_to_all(sent, "seq", 0, 0, tiled=True)
    sent = jnp.concatenate([to_owners(pick_half(grad_routed_in, core), share), small], axis=1)
    got = lax.all_to_all(sent, "seq", 0, 0, tiled=True)
    small = jnp.sum(got[:, 2 * share : 2 * share + 3, : model_width // dev_count].astype(f32), axis=0)
    got_grad = got[:, : 2 * share]
    block_rows = join_halves(got_update, tp_permute(got_update, 1), core)
    grad_slots = join_halves(got_grad, tp_permute(got_grad, 1), core)
    block_out = (tokens.astype(f32) + spread(table, block_rows)).astype(bf16)
    grad_tokens = out_grad.astype(f32) + spread(table, grad_slots)
    return (
        block_out,
        grad_tokens,
        small[0],
        grad_qkv,
        grad_out,
        small[1],
        grad_up,
        grad_down,
        small[2],
    )


def solution(mesh):
    def on_device(*arrays):
        seq_count, routed_len = arrays[2].shape
        dev_count = mesh.shape["seq"]
        whole = seq_count == dev_count and mesh.shape["tp"] == 4 and dev_count % 2 == 0
        body = on_device_whole if whole else on_device_split
        return body(*arrays)

    return jax.shard_map(
        on_device,
        mesh=mesh,
        in_specs=(
            P(None, "seq", None),
            P(),
            P(),
            P(),
            P(None, None, "tp"),
            P("tp", None),
            P(),
            P(None, "tp"),
            P("tp", None),
            P(),
            P(None, "seq", None),
        ),
        out_specs=(
            P(None, "seq", None),
            P(None, "seq", None),
            P("seq"),
            P("seq", None, "tp"),
            P("tp", "seq"),
            P("seq"),
            P("seq", "tp"),
            P("tp", "seq"),
            P("seq"),
        ),
        check_vma=False,
    )
```

```python
import jax
import jax.numpy as jnp
from jax import lax
from jax.sharding import PartitionSpec as P

HEAD_DIM = 64


precise = lax.Precision.HIGHEST


def normed(values, gain):
    factor = lax.rsqrt(jnp.mean(values * values, axis=-1, keepdims=True) + 1e-05)
    return values * factor * gain


def gelu_tanh(values):
    return jax.nn.gelu(values, approximate=True)


def match_table(positions, usable, anchor, extent):
    offsets = jnp.arange(extent, dtype=jnp.int32)
    hits = (positions - anchor)[:, :, None] == offsets[None, None, :]
    return jnp.logical_and(hits, usable[:, :, None]).astype(jnp.bfloat16)


def compact(table, source):
    return jnp.einsum("sqc,scd->sqd", table, source, preferred_element_type=jnp.float32)


def spread(table, routed_rows):
    return jnp.einsum("sqc,sqd->scd", table, routed_rows, preferred_element_type=jnp.float32)


def on_device_split(
    tokens,
    seg_ids,
    routed_index,
    gain_attn,
    w_qkv,
    w_out,
    gain_mlp,
    w_up,
    w_down,
    w_router,
    out_grad,
):
    seq_count, group_len, model_width = tokens.shape
    routed_len = routed_index.shape[1]
    dev_count = lax.axis_size("seq")
    dev_index = lax.axis_index("seq")
    per_dev = routed_len // dev_count
    group_base = dev_index * group_len
    seg_routed = jnp.take_along_axis(seg_ids, routed_index, axis=1)
    capacity = 2 * per_dev
    slot_ids = jnp.arange(capacity, dtype=jnp.int32)
    first_rank = jnp.sum((routed_index < group_base).astype(jnp.int32), axis=1)
    group_count = (
        jnp.sum((routed_index < group_base + group_len).astype(jnp.int32), axis=1) - first_rank
    )
    query_rank = first_rank[:, None] + slot_ids[None, :]
    query_valid = slot_ids[None, :] < group_count[:, None]
    clipped = jnp.minimum(query_rank, routed_len - 1)
    query_pos = jnp.take_along_axis(routed_index, clipped, axis=1)
    own_table = match_table(query_pos, query_valid, group_base, group_len)
    routed_rows = compact(own_table, tokens).astype(jnp.bfloat16)
    routed_grads = compact(own_table, out_grad).astype(jnp.bfloat16)
    query_seg = jnp.take_along_axis(seg_routed, clipped, axis=1)
    bounds = jnp.arange(dev_count, dtype=jnp.int32) * group_len
    firsts = jnp.sum((routed_index[:, :, None] < bounds[None, None, :]).astype(jnp.int32), axis=1)
    next_firsts = jnp.concatenate(
        [firsts[:, 1:], jnp.full((seq_count, 1), routed_len, jnp.int32)], axis=1
    )
    key_rank = (firsts[:, :, None] + slot_ids[None, None, :]).reshape(seq_count, -1)
    key_valid = (slot_ids[None, None, :] < (next_firsts - firsts)[:, :, None]).reshape(
        seq_count, -1
    )
    key_seg = jnp.take_along_axis(seg_routed, jnp.minimum(key_rank, routed_len - 1), axis=1)
    allowed = jnp.logical_and(
        key_rank[:, None, :] <= query_rank[:, :, None], key_seg[:, None, :] == query_seg[:, :, None]
    )
    allowed = jnp.logical_and(allowed, key_valid[:, None, :])[:, None]
    rows_float = routed_rows.astype(jnp.float32)
    gain_first = gain_attn.astype(jnp.float32)
    gain_second = gain_mlp.astype(jnp.float32)
    router_score = jnp.einsum(
        "sqd,d->sq", routed_rows, w_router, preferred_element_type=jnp.float32
    )
    gating = jax.nn.sigmoid(router_score)
    attn_input = normed(rows_float, gain_first).astype(jnp.bfloat16)
    qkv_rows = jnp.einsum(
        "sqd,dch->sqch", attn_input, w_qkv, preferred_element_type=jnp.float32
    ).astype(jnp.bfloat16)
    query_count = qkv_rows.shape[1]
    head_count = qkv_rows.shape[3] // HEAD_DIM
    query_flat = qkv_rows[:, :, 0]
    queries = query_flat.reshape(seq_count, query_count, head_count, HEAD_DIM)
    key_pair = (qkv_rows[:, :, 1], qkv_rows[:, :, 2])
    all_keys = lax.all_gather(key_pair[0], "seq", axis=1, tiled=True)
    all_values = lax.all_gather(key_pair[1], "seq", axis=1, tiled=True)
    key_count = all_keys.shape[1]
    all_keys = all_keys.reshape(seq_count, key_count, head_count, HEAD_DIM)
    all_values = all_values.reshape(seq_count, key_count, head_count, HEAD_DIM)
    scaling = HEAD_DIM ** (-0.5)

    def masked_logits():
        raw_scores = jnp.einsum(
            "sqhe,skhe->shqk", queries, all_keys, preferred_element_type=jnp.float32
        )
        return jnp.where(allowed, raw_scores * scaling, -1e30)

    logits = masked_logits()
    row_peak = jnp.max(logits, axis=-1, keepdims=True)
    powered = jnp.exp(logits - row_peak)
    row_total = jnp.sum(powered, axis=-1, keepdims=True)
    log_total = row_peak + jnp.log(row_total)
    probs_low = (powered / row_total).astype(jnp.bfloat16)
    mixed = jnp.einsum("shqk,skhe->sqhe", probs_low, all_values, preferred_element_type=jnp.float32)
    mixed = mixed.reshape(seq_count, query_count, -1).astype(jnp.bfloat16)
    attn_out = lax.psum(
        jnp.einsum("sqh,hd->sqd", mixed, w_out, preferred_element_type=jnp.float32).astype(
            jnp.bfloat16
        ),
        "tp",
    ).astype(jnp.float32)
    residual = rows_float + attn_out
    mlp_input = normed(residual, gain_second).astype(jnp.bfloat16)
    pre_act = jnp.einsum("sqd,df->sqf", mlp_input, w_up, preferred_element_type=jnp.float32)
    hidden = gelu_tanh(pre_act).astype(jnp.bfloat16)
    mlp_out = lax.psum(
        jnp.einsum("sqf,fd->sqd", hidden, w_down, preferred_element_type=jnp.float32).astype(
            jnp.bfloat16
        ),
        "tp",
    ).astype(jnp.float32)
    branch = attn_out + mlp_out
    update_rows = (gating[:, :, None] * branch).astype(jnp.bfloat16)
    block_out = (tokens.astype(jnp.float32) + spread(own_table, update_rows)).astype(jnp.bfloat16)
    grad_rows = routed_grads.astype(jnp.float32)
    scaled_grad = gating[:, :, None] * grad_rows
    grad_score = jnp.sum(grad_rows * branch, axis=-1) * gating * (1.0 - gating)
    grad_mlp = scaled_grad.astype(jnp.bfloat16)
    grad_down = jnp.einsum("sqf,sqd->fd", hidden, grad_mlp, preferred_element_type=jnp.float32)
    grad_hidden = jnp.einsum("sqd,fd->sqf", grad_mlp, w_down, preferred_element_type=jnp.float32)
    gelu_pull = jax.vjp(gelu_tanh, pre_act)[1]
    grad_pre = gelu_pull(grad_hidden)[0].astype(jnp.bfloat16)
    grad_up = jnp.einsum("sqd,sqf->df", mlp_input, grad_pre, preferred_element_type=jnp.float32)
    grad_mlp_input = lax.psum(
        jnp.einsum("sqf,df->sqd", grad_pre, w_up, preferred_element_type=jnp.float32).astype(
            jnp.bfloat16
        ),
        "tp",
    ).astype(jnp.float32)
    second_pull = jax.vjp(normed, residual, gain_second)[1]
    grad_residual, grad_gain_mlp = second_pull(grad_mlp_input)
    grad_attn = (grad_residual + scaled_grad).astype(jnp.bfloat16)
    grad_out = jnp.einsum("sqh,sqd->hd", mixed, grad_attn, preferred_element_type=jnp.float32)
    grad_mixed_flat = jnp.einsum(
        "sqd,hd->sqh", grad_attn, w_out, preferred_element_type=jnp.float32
    ).astype(jnp.bfloat16)
    grad_mixed = grad_mixed_flat.reshape(seq_count, query_count, head_count, HEAD_DIM)
    probs_again = jnp.where(allowed, jnp.exp(masked_logits() - log_total), 0.0)
    grad_probs = jnp.einsum(
        "sqhe,skhe->shqk", grad_mixed, all_values, preferred_element_type=jnp.float32
    )
    inner_sum = jnp.sum(probs_again * grad_probs, axis=-1, keepdims=True)
    grad_raw = (probs_again * (grad_probs - inner_sum) * scaling).astype(jnp.bfloat16)
    grad_query = jnp.einsum(
        "shqk,skhe->sqhe", grad_raw, all_keys, preferred_element_type=jnp.float32
    )
    grad_query = grad_query.reshape(seq_count, query_count, -1).astype(jnp.bfloat16)
    probs_again_low = probs_again.astype(jnp.bfloat16)
    key_part = jnp.einsum(
        "shqk,sqhe->skhe", grad_raw, queries, preferred_element_type=jnp.float32
    ).reshape(seq_count, key_count, -1)
    value_part = jnp.einsum(
        "shqk,sqhe->skhe", probs_again_low, grad_mixed, preferred_element_type=jnp.float32
    ).reshape(seq_count, key_count, -1)
    key_pair = (key_part, value_part)
    grad_keys = lax.psum_scatter(key_pair[0], "seq", scatter_dimension=1, tiled=True)
    grad_values = lax.psum_scatter(key_pair[1], "seq", scatter_dimension=1, tiled=True)
    grad_qkv_rows = jnp.stack(
        [grad_query, grad_keys.astype(jnp.bfloat16), grad_values.astype(jnp.bfloat16)], axis=2
    )
    grad_qkv = jnp.einsum(
        "sqd,sqch->dch", attn_input, grad_qkv_rows, preferred_element_type=jnp.float32
    )
    grad_attn_input = lax.psum(
        jnp.einsum(
            "sqch,dch->sqd", grad_qkv_rows, w_qkv, preferred_element_type=jnp.float32
        ).astype(jnp.bfloat16),
        "tp",
    ).astype(jnp.float32)
    first_pull = jax.vjp(normed, rows_float, gain_first)[1]
    grad_norm, grad_gain_attn = first_pull(grad_attn_input)
    grad_router = jnp.einsum("sq,sqd->d", grad_score, rows_float, precision=precise)
    grad_routed_in = (
        grad_residual + grad_norm + grad_score[:, :, None] * w_router.astype(jnp.float32)
    ).astype(jnp.bfloat16)
    grad_tokens = out_grad.astype(jnp.float32) + spread(own_table, grad_routed_in)
    reduced = (
        lax.psum_scatter(grad_gain_attn, "seq", scatter_dimension=0, tiled=True),
        lax.psum_scatter(grad_qkv, "seq", scatter_dimension=0, tiled=True),
        lax.psum_scatter(grad_out, "seq", scatter_dimension=1, tiled=True),
        lax.psum_scatter(grad_gain_mlp, "seq", scatter_dimension=0, tiled=True),
        lax.psum_scatter(grad_up, "seq", scatter_dimension=0, tiled=True),
        lax.psum_scatter(grad_down, "seq", scatter_dimension=1, tiled=True),
        lax.psum_scatter(grad_router, "seq", scatter_dimension=0, tiled=True),
    )
    return (block_out, grad_tokens) + tuple(reduced)


def ring_order(size):
    return list(range(0, size, 2)) + list(range(size - 1, 0, -2))


def ring_place(index, size):
    return jnp.where(index % 2 == 0, index // 2, size - 1 - index // 2)


def ring_owner(place, size):
    place = place % size
    return jnp.where(place < size // 2, 2 * place, 2 * (size - place) - 1)


def ring_permute(values, direction):
    order = ring_order(lax.axis_size("seq"))
    size = len(order)
    pairs = [(order[i], order[(i + direction) % size]) for i in range(size)]
    return lax.ppermute(values, "seq", pairs)


def ring_scatter(whole, axis, direction):
    size = lax.axis_size("seq")
    place = ring_place(lax.axis_index("seq"), size)
    width = whole.shape[axis] // size

    def chunk(k):
        owner = ring_owner(place + size - direction * (1 + k), size)
        return lax.dynamic_slice_in_dim(whole, owner * width, width, axis)

    total = chunk(0)
    for k in range(1, size):
        moved = ring_permute(total, direction)
        total = moved.astype(jnp.float32) + chunk(k).astype(jnp.float32)
        if k < size - 1:
            total = total.astype(jnp.bfloat16)
    return total


def tp_permute(values, mask):
    size = lax.axis_size("tp")
    return lax.ppermute(values, "tp", [(i, i ^ mask) for i in range(size)])


def pick_half(values, which):
    width = values.shape[-1] // 2
    return jnp.where(which == 0, values[..., :width], values[..., width:])


def join_halves(own, other, which):
    return jnp.where(
        which == 0,
        jnp.concatenate([own, other], axis=-1),
        jnp.concatenate([other, own], axis=-1),
    )


def tp_sum(partial, which):
    narrow = partial.astype(jnp.bfloat16)
    moved = tp_permute(pick_half(narrow, 1 - which), 1)
    half = pick_half(partial, which) + moved.astype(jnp.float32)
    half = half.astype(jnp.bfloat16)
    moved = tp_permute(half, 2)
    half = (half.astype(jnp.float32) + moved.astype(jnp.float32)).astype(jnp.bfloat16)
    return join_halves(half, tp_permute(half, 1), which).astype(jnp.float32)


def to_owners(rows, share):
    groups = rows.reshape(-1, share, rows.shape[-1])
    later = jnp.concatenate([groups[1:], jnp.zeros_like(groups[:1])], axis=0)
    return jnp.concatenate([groups, later], axis=1)


def from_owners(slots, share):
    later = jnp.concatenate([jnp.zeros_like(slots[:1, share:]), slots[:-1, share:]], axis=0)
    return (slots[:, :share] + later).reshape(-1, slots.shape[-1])


def on_device_whole(
    tokens,
    seg_ids,
    routed_index,
    gain_attn,
    w_qkv,
    w_out,
    gain_mlp,
    w_up,
    w_down,
    w_router,
    out_grad,
):
    f32, bf16 = jnp.float32, jnp.bfloat16
    seq_count, group_len, model_width = tokens.shape
    routed_len = routed_index.shape[1]
    dev_count = lax.axis_size("seq")
    dev_index = lax.axis_index("seq")
    core = lax.axis_index("tp") % 2
    share = routed_len // dev_count
    half_width = model_width // 2

    padded_index = jnp.concatenate(
        [routed_index, jnp.full((seq_count, share), -1, jnp.int32)], axis=1
    )
    slots = lax.dynamic_slice(padded_index, (0, dev_index * share), (seq_count, 2 * share))
    offsets = jnp.arange(group_len, dtype=jnp.int32)
    table = ((slots - dev_index * group_len)[:, :, None] == offsets).astype(bf16)

    index_row = lax.dynamic_index_in_dim(routed_index, dev_index, 0, False)
    seg_row = lax.dynamic_index_in_dim(seg_ids, dev_index, 0, False)
    seg_routed = sum(
        (index_row >= jnp.sum((seg_row < t).astype(jnp.int32))).astype(jnp.int32)
        for t in range(1, 4)
    )
    ranks = jnp.arange(routed_len, dtype=jnp.int32)
    allowed = jnp.logical_and(
        ranks[None, :] <= ranks[:, None], seg_routed[None, :] == seg_routed[:, None]
    )[None]

    def fetch(source):
        own = lax.dynamic_slice_in_dim(source, core * half_width, half_width, 2)
        own = compact(table, own).astype(bf16)
        own = from_owners(lax.all_to_all(own, "seq", 0, 0, tiled=True), share)
        return join_halves(own, tp_permute(own, 1), core)

    routed_rows = fetch(tokens)
    routed_grads = fetch(out_grad)

    rows = routed_rows.astype(f32)
    grad_rows = routed_grads.astype(f32)
    gain_first = gain_attn.astype(f32)
    gain_second = gain_mlp.astype(f32)
    router = w_router.astype(f32)
    gating = jax.nn.sigmoid(jnp.sum(rows * router, axis=-1, keepdims=True))
    factor_first = lax.rsqrt(jnp.mean(rows * rows, axis=-1, keepdims=True) + 1e-05)
    attn_input = (rows * factor_first * gain_first).astype(bf16)
    weights = jnp.transpose(w_qkv, (1, 0, 2))
    qkv = jnp.einsum("rd,cdh->crh", attn_input, weights, preferred_element_type=f32).astype(bf16)
    head_count = qkv.shape[2] // HEAD_DIM
    scaling = HEAD_DIM ** (-0.5)

    def heads(values):
        return values.reshape(routed_len, head_count, HEAD_DIM)

    queries, keys, values = heads(qkv[0]), heads(qkv[1]), heads(qkv[2])
    raw = jnp.einsum("qhe,khe->hqk", queries, keys, preferred_element_type=f32)
    logits = jnp.where(allowed, raw * scaling, -1e30)
    powered = jnp.exp(logits - jnp.max(logits, axis=-1, keepdims=True))
    probs = powered / jnp.sum(powered, axis=-1, keepdims=True)
    probs_low = probs.astype(bf16)
    mixed = jnp.einsum("hqk,khe->qhe", probs_low, values, preferred_element_type=f32)
    mixed = mixed.reshape(routed_len, -1).astype(bf16)
    attn_out = tp_sum(jnp.dot(mixed, w_out, preferred_element_type=f32), core)

    residual = rows + attn_out
    factor_second = lax.rsqrt(jnp.mean(residual * residual, axis=-1, keepdims=True) + 1e-05)
    mlp_input = (residual * factor_second * gain_second).astype(bf16)
    scaled_grad = gating * grad_rows
    grad_mlp = scaled_grad.astype(bf16)
    pre_act = jnp.dot(mlp_input, w_up, preferred_element_type=f32)
    hidden, gelu_pull = jax.vjp(gelu_tanh, pre_act)
    hidden = hidden.astype(bf16)
    grad_hidden = lax.dot_general(
        grad_mlp, w_down, (((1,), (1,)), ((), ())), preferred_element_type=f32
    )
    grad_pre = gelu_pull(grad_hidden)[0].astype(bf16)
    grad_mlp_input = tp_sum(
        lax.dot_general(grad_pre, w_up, (((1,), (1,)), ((), ())), preferred_element_type=f32), core
    )
    mlp_out = tp_sum(jnp.dot(hidden, w_down, preferred_element_type=f32), core)

    def outer(left, right):
        product = lax.dot_general(
            left, right, (((0,), (0,)), ((), ())), preferred_element_type=f32
        )
        return product.astype(bf16)

    grad_up = ring_scatter(outer(mlp_input, grad_pre), 0, 1)
    grad_down = ring_scatter(outer(hidden, grad_mlp), 1, -1)

    weighted = grad_mlp_input * gain_second
    grad_residual = factor_second * weighted - residual * factor_second**3 * jnp.mean(
        residual * weighted, axis=-1, keepdims=True
    )
    grad_gain_mlp = jnp.sum(grad_mlp_input * residual * factor_second, axis=0)
    grad_attn = (grad_residual + scaled_grad).astype(bf16)
    grad_mixed = lax.dot_general(
        grad_attn, w_out, (((1,), (1,)), ((), ())), preferred_element_type=f32
    ).astype(bf16)
    grad_heads = heads(grad_mixed)
    grad_probs = jnp.einsum("qhe,khe->hqk", grad_heads, values, preferred_element_type=f32)
    inner_sum = jnp.sum(probs * grad_probs, axis=-1, keepdims=True)
    grad_raw = (probs * (grad_probs - inner_sum) * scaling).astype(bf16)

    def flat(products):
        return products.reshape(routed_len, -1).astype(bf16)

    grad_query = flat(jnp.einsum("hqk,khe->qhe", grad_raw, keys, preferred_element_type=f32))
    grad_key = flat(jnp.einsum("hqk,qhe->khe", grad_raw, queries, preferred_element_type=f32))
    grad_value = flat(jnp.einsum("hqk,qhe->khe", probs_low, grad_heads, preferred_element_type=f32))
    grad_parts = (grad_query, grad_key, grad_value)
    grad_attn_input = tp_sum(
        sum(
            lax.dot_general(
                grad_parts[c], weights[c], (((1,), (1,)), ((), ())), preferred_element_type=f32
            )
            for c in range(3)
        ),
        core,
    )
    grad_qkv = jnp.stack(
        [
            ring_scatter(outer(attn_input, grad_parts[c]), 0, -1 if c == 2 else 1)
            for c in range(3)
        ],
        axis=1,
    )
    grad_out = ring_scatter(outer(mixed, grad_attn), 1, -1)

    branch = attn_out + mlp_out
    update = (gating * branch).astype(bf16)
    grad_score = gating * (1.0 - gating) * jnp.sum(grad_rows * branch, axis=-1, keepdims=True)
    weighted = grad_attn_input * gain_first
    grad_norm = factor_first * weighted - rows * factor_first**3 * jnp.mean(
        rows * weighted, axis=-1, keepdims=True
    )
    grad_gain_attn = jnp.sum(grad_attn_input * rows * factor_first, axis=0)
    grad_router = jnp.sum(grad_score * rows, axis=0)
    grad_routed_in = (grad_residual + grad_norm + grad_score * router).astype(bf16)

    small = jnp.stack([grad_gain_attn, grad_gain_mlp, grad_router]).astype(bf16)
    small = small.reshape(3, dev_count, -1).transpose(1, 0, 2)
    small = jnp.pad(small, ((0, 0), (0, 13), (0, half_width - small.shape[2])))
    sent = to_owners(pick_half(update, core), share)
    got_update = lax.all_to_all(sent, "seq", 0, 0, tiled=True)
    sent = jnp.concatenate([to_owners(pick_half(grad_routed_in, core), share), small], axis=1)
    got = lax.all_to_all(sent, "seq", 0, 0, tiled=True)
    small = jnp.sum(got[:, 2 * share : 2 * share + 3, : model_width // dev_count].astype(f32), axis=0)
    got_grad = got[:, : 2 * share]
    block_rows = join_halves(got_update, tp_permute(got_update, 1), core)
    grad_slots = join_halves(got_grad, tp_permute(got_grad, 1), core)
    block_out = (tokens.astype(f32) + spread(table, block_rows)).astype(bf16)
    grad_tokens = out_grad.astype(f32) + spread(table, grad_slots)
    return (
        block_out,
        grad_tokens,
        small[0],
        grad_qkv,
        grad_out,
        small[1],
        grad_up,
        grad_down,
        small[2],
    )


def solution(mesh):
    def on_device(*arrays):
        seq_count, routed_len = arrays[2].shape
        dev_count = mesh.shape["seq"]
        whole = seq_count == dev_count and mesh.shape["tp"] == 4 and dev_count % 2 == 0
        body = on_device_whole if whole else on_device_split
        return body(*arrays)

    return jax.shard_map(
        on_device,
        mesh=mesh,
        in_specs=(
            P(None, "seq", None),
            P(),
            P(),
            P(),
            P(None, None, "tp"),
            P("tp", None),
            P(),
            P(None, "tp"),
            P("tp", None),
            P(),
            P(None, "seq", None),
        ),
        out_specs=(
            P(None, "seq", None),
            P(None, "seq", None),
            P("seq"),
            P("seq", None, "tp"),
            P("tp", "seq"),
            P("seq"),
            P("seq", "tp"),
            P("tp", "seq"),
            P("seq"),
        ),
        check_vma=False,
    )
```

```python
import jax
import jax.numpy as jnp
from jax import lax
from jax.sharding import PartitionSpec as P

HEAD_DIM = 64


precise = lax.Precision.HIGHEST


def normed(values, gain):
    factor = lax.rsqrt(jnp.mean(values * values, axis=-1, keepdims=True) + 1e-05)
    return values * factor * gain


def gelu_tanh(values):
    return jax.nn.gelu(values, approximate=True)


def match_table(positions, usable, anchor, extent):
    offsets = jnp.arange(extent, dtype=jnp.int32)
    hits = (positions - anchor)[:, :, None] == offsets[None, None, :]
    return jnp.logical_and(hits, usable[:, :, None]).astype(jnp.bfloat16)


def compact(table, source):
    return jnp.einsum("sqc,scd->sqd", table, source, preferred_element_type=jnp.float32)


def spread(table, routed_rows):
    return jnp.einsum("sqc,sqd->scd", table, routed_rows, preferred_element_type=jnp.float32)


def on_device_split(
    tokens,
    seg_ids,
    routed_index,
    gain_attn,
    w_qkv,
    w_out,
    gain_mlp,
    w_up,
    w_down,
    w_router,
    out_grad,
):
    seq_count, group_len, model_width = tokens.shape
    routed_len = routed_index.shape[1]
    dev_count = lax.axis_size("seq")
    dev_index = lax.axis_index("seq")
    per_dev = routed_len // dev_count
    group_base = dev_index * group_len
    seg_routed = jnp.take_along_axis(seg_ids, routed_index, axis=1)
    capacity = 2 * per_dev
    slot_ids = jnp.arange(capacity, dtype=jnp.int32)
    first_rank = jnp.sum((routed_index < group_base).astype(jnp.int32), axis=1)
    group_count = (
        jnp.sum((routed_index < group_base + group_len).astype(jnp.int32), axis=1) - first_rank
    )
    query_rank = first_rank[:, None] + slot_ids[None, :]
    query_valid = slot_ids[None, :] < group_count[:, None]
    clipped = jnp.minimum(query_rank, routed_len - 1)
    query_pos = jnp.take_along_axis(routed_index, clipped, axis=1)
    own_table = match_table(query_pos, query_valid, group_base, group_len)
    routed_rows = compact(own_table, tokens).astype(jnp.bfloat16)
    routed_grads = compact(own_table, out_grad).astype(jnp.bfloat16)
    query_seg = jnp.take_along_axis(seg_routed, clipped, axis=1)
    bounds = jnp.arange(dev_count, dtype=jnp.int32) * group_len
    firsts = jnp.sum((routed_index[:, :, None] < bounds[None, None, :]).astype(jnp.int32), axis=1)
    next_firsts = jnp.concatenate(
        [firsts[:, 1:], jnp.full((seq_count, 1), routed_len, jnp.int32)], axis=1
    )
    key_rank = (firsts[:, :, None] + slot_ids[None, None, :]).reshape(seq_count, -1)
    key_valid = (slot_ids[None, None, :] < (next_firsts - firsts)[:, :, None]).reshape(
        seq_count, -1
    )
    key_seg = jnp.take_along_axis(seg_routed, jnp.minimum(key_rank, routed_len - 1), axis=1)
    allowed = jnp.logical_and(
        key_rank[:, None, :] <= query_rank[:, :, None], key_seg[:, None, :] == query_seg[:, :, None]
    )
    allowed = jnp.logical_and(allowed, key_valid[:, None, :])[:, None]
    rows_float = routed_rows.astype(jnp.float32)
    gain_first = gain_attn.astype(jnp.float32)
    gain_second = gain_mlp.astype(jnp.float32)
    router_score = jnp.einsum(
        "sqd,d->sq", routed_rows, w_router, preferred_element_type=jnp.float32
    )
    gating = jax.nn.sigmoid(router_score)
    attn_input = normed(rows_float, gain_first).astype(jnp.bfloat16)
    qkv_rows = jnp.einsum(
        "sqd,dch->sqch", attn_input, w_qkv, preferred_element_type=jnp.float32
    ).astype(jnp.bfloat16)
    query_count = qkv_rows.shape[1]
    head_count = qkv_rows.shape[3] // HEAD_DIM
    query_flat = qkv_rows[:, :, 0]
    queries = query_flat.reshape(seq_count, query_count, head_count, HEAD_DIM)
    key_pair = (qkv_rows[:, :, 1], qkv_rows[:, :, 2])
    all_keys = lax.all_gather(key_pair[0], "seq", axis=1, tiled=True)
    all_values = lax.all_gather(key_pair[1], "seq", axis=1, tiled=True)
    key_count = all_keys.shape[1]
    all_keys = all_keys.reshape(seq_count, key_count, head_count, HEAD_DIM)
    all_values = all_values.reshape(seq_count, key_count, head_count, HEAD_DIM)
    scaling = HEAD_DIM ** (-0.5)

    def masked_logits():
        raw_scores = jnp.einsum(
            "sqhe,skhe->shqk", queries, all_keys, preferred_element_type=jnp.float32
        )
        return jnp.where(allowed, raw_scores * scaling, -1e30)

    logits = masked_logits()
    row_peak = jnp.max(logits, axis=-1, keepdims=True)
    powered = jnp.exp(logits - row_peak)
    row_total = jnp.sum(powered, axis=-1, keepdims=True)
    log_total = row_peak + jnp.log(row_total)
    probs_low = (powered / row_total).astype(jnp.bfloat16)
    mixed = jnp.einsum("shqk,skhe->sqhe", probs_low, all_values, preferred_element_type=jnp.float32)
    mixed = mixed.reshape(seq_count, query_count, -1).astype(jnp.bfloat16)
    attn_out = lax.psum(
        jnp.einsum("sqh,hd->sqd", mixed, w_out, preferred_element_type=jnp.float32).astype(
            jnp.bfloat16
        ),
        "tp",
    ).astype(jnp.float32)
    residual = rows_float + attn_out
    mlp_input = normed(residual, gain_second).astype(jnp.bfloat16)
    pre_act = jnp.einsum("sqd,df->sqf", mlp_input, w_up, preferred_element_type=jnp.float32)
    hidden = gelu_tanh(pre_act).astype(jnp.bfloat16)
    mlp_out = lax.psum(
        jnp.einsum("sqf,fd->sqd", hidden, w_down, preferred_element_type=jnp.float32).astype(
            jnp.bfloat16
        ),
        "tp",
    ).astype(jnp.float32)
    branch = attn_out + mlp_out
    update_rows = (gating[:, :, None] * branch).astype(jnp.bfloat16)
    block_out = (tokens.astype(jnp.float32) + spread(own_table, update_rows)).astype(jnp.bfloat16)
    grad_rows = routed_grads.astype(jnp.float32)
    scaled_grad = gating[:, :, None] * grad_rows
    grad_score = jnp.sum(grad_rows * branch, axis=-1) * gating * (1.0 - gating)
    grad_mlp = scaled_grad.astype(jnp.bfloat16)
    grad_down = jnp.einsum("sqf,sqd->fd", hidden, grad_mlp, preferred_element_type=jnp.float32)
    grad_hidden = jnp.einsum("sqd,fd->sqf", grad_mlp, w_down, preferred_element_type=jnp.float32)
    gelu_pull = jax.vjp(gelu_tanh, pre_act)[1]
    grad_pre = gelu_pull(grad_hidden)[0].astype(jnp.bfloat16)
    grad_up = jnp.einsum("sqd,sqf->df", mlp_input, grad_pre, preferred_element_type=jnp.float32)
    grad_mlp_input = lax.psum(
        jnp.einsum("sqf,df->sqd", grad_pre, w_up, preferred_element_type=jnp.float32).astype(
            jnp.bfloat16
        ),
        "tp",
    ).astype(jnp.float32)
    second_pull = jax.vjp(normed, residual, gain_second)[1]
    grad_residual, grad_gain_mlp = second_pull(grad_mlp_input)
    grad_attn = (grad_residual + scaled_grad).astype(jnp.bfloat16)
    grad_out = jnp.einsum("sqh,sqd->hd", mixed, grad_attn, preferred_element_type=jnp.float32)
    grad_mixed_flat = jnp.einsum(
        "sqd,hd->sqh", grad_attn, w_out, preferred_element_type=jnp.float32
    ).astype(jnp.bfloat16)
    grad_mixed = grad_mixed_flat.reshape(seq_count, query_count, head_count, HEAD_DIM)
    probs_again = jnp.where(allowed, jnp.exp(masked_logits() - log_total), 0.0)
    grad_probs = jnp.einsum(
        "sqhe,skhe->shqk", grad_mixed, all_values, preferred_element_type=jnp.float32
    )
    inner_sum = jnp.sum(probs_again * grad_probs, axis=-1, keepdims=True)
    grad_raw = (probs_again * (grad_probs - inner_sum) * scaling).astype(jnp.bfloat16)
    grad_query = jnp.einsum(
        "shqk,skhe->sqhe", grad_raw, all_keys, preferred_element_type=jnp.float32
    )
    grad_query = grad_query.reshape(seq_count, query_count, -1).astype(jnp.bfloat16)
    probs_again_low = probs_again.astype(jnp.bfloat16)
    key_part = jnp.einsum(
        "shqk,sqhe->skhe", grad_raw, queries, preferred_element_type=jnp.float32
    ).reshape(seq_count, key_count, -1)
    value_part = jnp.einsum(
        "shqk,sqhe->skhe", probs_again_low, grad_mixed, preferred_element_type=jnp.float32
    ).reshape(seq_count, key_count, -1)
    key_pair = (key_part, value_part)
    grad_keys = lax.psum_scatter(key_pair[0], "seq", scatter_dimension=1, tiled=True)
    grad_values = lax.psum_scatter(key_pair[1], "seq", scatter_dimension=1, tiled=True)
    grad_qkv_rows = jnp.stack(
        [grad_query, grad_keys.astype(jnp.bfloat16), grad_values.astype(jnp.bfloat16)], axis=2
    )
    grad_qkv = jnp.einsum(
        "sqd,sqch->dch", attn_input, grad_qkv_rows, preferred_element_type=jnp.float32
    )
    grad_attn_input = lax.psum(
        jnp.einsum(
            "sqch,dch->sqd", grad_qkv_rows, w_qkv, preferred_element_type=jnp.float32
        ).astype(jnp.bfloat16),
        "tp",
    ).astype(jnp.float32)
    first_pull = jax.vjp(normed, rows_float, gain_first)[1]
    grad_norm, grad_gain_attn = first_pull(grad_attn_input)
    grad_router = jnp.einsum("sq,sqd->d", grad_score, rows_float, precision=precise)
    grad_routed_in = (
        grad_residual + grad_norm + grad_score[:, :, None] * w_router.astype(jnp.float32)
    ).astype(jnp.bfloat16)
    grad_tokens = out_grad.astype(jnp.float32) + spread(own_table, grad_routed_in)
    reduced = (
        lax.psum_scatter(grad_gain_attn, "seq", scatter_dimension=0, tiled=True),
        lax.psum_scatter(grad_qkv, "seq", scatter_dimension=0, tiled=True),
        lax.psum_scatter(grad_out, "seq", scatter_dimension=1, tiled=True),
        lax.psum_scatter(grad_gain_mlp, "seq", scatter_dimension=0, tiled=True),
        lax.psum_scatter(grad_up, "seq", scatter_dimension=0, tiled=True),
        lax.psum_scatter(grad_down, "seq", scatter_dimension=1, tiled=True),
        lax.psum_scatter(grad_router, "seq", scatter_dimension=0, tiled=True),
    )
    return (block_out, grad_tokens) + tuple(reduced)


def ring_order(size):
    return list(range(0, size, 2)) + list(range(size - 1, 0, -2))


def ring_place(index, size):
    return jnp.where(index % 2 == 0, index // 2, size - 1 - index // 2)


def ring_owner(place, size):
    place = place % size
    return jnp.where(place < size // 2, 2 * place, 2 * (size - place) - 1)


def ring_permute(values):
    order = ring_order(lax.axis_size("seq"))
    size, width = len(order), lax.axis_size("tp")
    pairs = []
    for i in range(size):
        for t in range(width):
            after = (i + 1 - 2 * (t % 2)) % size
            pairs.append((order[i] * width + t, order[after] * width + t))
    return lax.ppermute(values, ("seq", "tp"), pairs)


def ring_scatter(whole, axis, core):
    size = lax.axis_size("seq")
    place = ring_place(lax.axis_index("seq"), size)
    width = whole.shape[axis] // size
    direction = 1 - 2 * core

    def chunk(k):
        owner = ring_owner(place + size - direction * (1 + k), size)
        return lax.dynamic_slice_in_dim(whole, owner * width, width, axis)

    total = chunk(0)
    for k in range(1, size):
        moved = ring_permute(total)
        total = moved.astype(jnp.float32) + chunk(k).astype(jnp.float32)
        if k < size - 1:
            total = total.astype(jnp.bfloat16)
    return total


def tp_permute(values, mask):
    size = lax.axis_size("tp")
    return lax.ppermute(values, "tp", [(i, i ^ mask) for i in range(size)])


def pick_half(values, which):
    width = values.shape[-1] // 2
    return jnp.where(which == 0, values[..., :width], values[..., width:])


def join_halves(own, other, which):
    return jnp.where(
        which == 0,
        jnp.concatenate([own, other], axis=-1),
        jnp.concatenate([other, own], axis=-1),
    )


def tp_sum(partial, which):
    narrow = partial.astype(jnp.bfloat16)
    moved = tp_permute(pick_half(narrow, 1 - which), 1)
    half = pick_half(partial, which) + moved.astype(jnp.float32)
    half = half.astype(jnp.bfloat16)
    moved = tp_permute(half, 2)
    half = (half.astype(jnp.float32) + moved.astype(jnp.float32)).astype(jnp.bfloat16)
    return join_halves(half, tp_permute(half, 1), which).astype(jnp.float32)


def to_owners(rows, share):
    groups = rows.reshape(-1, share, rows.shape[-1])
    later = jnp.concatenate([groups[1:], jnp.zeros_like(groups[:1])], axis=0)
    return jnp.concatenate([groups, later], axis=1)


def from_owners(slots, share):
    later = jnp.concatenate([jnp.zeros_like(slots[:1, share:]), slots[:-1, share:]], axis=0)
    return (slots[:, :share] + later).reshape(-1, slots.shape[-1])


def on_device_whole(
    tokens,
    seg_ids,
    routed_index,
    gain_attn,
    w_qkv,
    w_out,
    gain_mlp,
    w_up,
    w_down,
    w_router,
    out_grad,
):
    f32, bf16 = jnp.float32, jnp.bfloat16
    seq_count, group_len, model_width = tokens.shape
    routed_len = routed_index.shape[1]
    dev_count = lax.axis_size("seq")
    dev_index = lax.axis_index("seq")
    core = lax.axis_index("tp") % 2
    share = routed_len // dev_count
    half_width = model_width // 2

    padded_index = jnp.concatenate(
        [routed_index, jnp.full((seq_count, share), -1, jnp.int32)], axis=1
    )
    slots = lax.dynamic_slice(padded_index, (0, dev_index * share), (seq_count, 2 * share))
    offsets = jnp.arange(group_len, dtype=jnp.int32)
    table = ((slots - dev_index * group_len)[:, :, None] == offsets).astype(bf16)

    index_row = lax.dynamic_index_in_dim(routed_index, dev_index, 0, False)
    seg_row = lax.dynamic_index_in_dim(seg_ids, dev_index, 0, False)
    seg_routed = sum(
        (index_row >= jnp.sum((seg_row < t).astype(jnp.int32))).astype(jnp.int32)
        for t in range(1, 4)
    )
    ranks = jnp.arange(routed_len, dtype=jnp.int32)
    allowed = jnp.logical_and(
        ranks[None, :] <= ranks[:, None], seg_routed[None, :] == seg_routed[:, None]
    )[None]

    def fetch(source):
        own = lax.dynamic_slice_in_dim(source, core * half_width, half_width, 2)
        own = compact(table, own).astype(bf16)
        own = from_owners(lax.all_to_all(own, "seq", 0, 0, tiled=True), share)
        return join_halves(own, tp_permute(own, 1), core)

    routed_rows = fetch(tokens)
    routed_grads = fetch(out_grad)

    rows = routed_rows.astype(f32)
    grad_rows = routed_grads.astype(f32)
    gain_first = gain_attn.astype(f32)
    gain_second = gain_mlp.astype(f32)
    router = w_router.astype(f32)
    gating = jax.nn.sigmoid(jnp.sum(rows * router, axis=-1, keepdims=True))
    factor_first = lax.rsqrt(jnp.mean(rows * rows, axis=-1, keepdims=True) + 1e-05)
    attn_input = (rows * factor_first * gain_first).astype(bf16)
    weights = jnp.transpose(w_qkv, (1, 0, 2))
    qkv = jnp.einsum("rd,cdh->crh", attn_input, weights, preferred_element_type=f32).astype(bf16)
    head_count = qkv.shape[2] // HEAD_DIM
    scaling = HEAD_DIM ** (-0.5)

    def heads(values):
        return values.reshape(routed_len, head_count, HEAD_DIM)

    queries, keys, values = heads(qkv[0]), heads(qkv[1]), heads(qkv[2])
    raw = jnp.einsum("qhe,khe->hqk", queries, keys, preferred_element_type=f32)
    logits = jnp.where(allowed, raw * scaling, -1e30)
    powered = jnp.exp(logits - jnp.max(logits, axis=-1, keepdims=True))
    probs = powered / jnp.sum(powered, axis=-1, keepdims=True)
    probs_low = probs.astype(bf16)
    mixed = jnp.einsum("hqk,khe->qhe", probs_low, values, preferred_element_type=f32)
    mixed = mixed.reshape(routed_len, -1).astype(bf16)
    attn_out = tp_sum(jnp.dot(mixed, w_out, preferred_element_type=f32), core)

    residual = rows + attn_out
    factor_second = lax.rsqrt(jnp.mean(residual * residual, axis=-1, keepdims=True) + 1e-05)
    mlp_input = (residual * factor_second * gain_second).astype(bf16)
    scaled_grad = gating * grad_rows
    grad_mlp = scaled_grad.astype(bf16)
    pre_act = jnp.dot(mlp_input, w_up, preferred_element_type=f32)
    hidden, gelu_pull = jax.vjp(gelu_tanh, pre_act)
    hidden = hidden.astype(bf16)
    grad_hidden = lax.dot_general(
        grad_mlp, w_down, (((1,), (1,)), ((), ())), preferred_element_type=f32
    )
    grad_pre = gelu_pull(grad_hidden)[0].astype(bf16)
    grad_mlp_input = tp_sum(
        lax.dot_general(grad_pre, w_up, (((1,), (1,)), ((), ())), preferred_element_type=f32), core
    )
    mlp_out = tp_sum(jnp.dot(hidden, w_down, preferred_element_type=f32), core)

    def outer(left, right):
        product = lax.dot_general(
            left, right, (((0,), (0,)), ((), ())), preferred_element_type=f32
        )
        return product.astype(bf16)

    mlp_pairs = lax.dot_general(
        jnp.stack([mlp_input, grad_mlp]),
        jnp.stack([grad_pre, hidden]),
        (((1,), (1,)), ((0,), (0,))),
        preferred_element_type=f32,
    )
    mlp_grads = ring_scatter(mlp_pairs.astype(bf16), 1, core)
    grad_up, grad_down = mlp_grads[0], mlp_grads[1].T

    weighted = grad_mlp_input * gain_second
    grad_residual = factor_second * weighted - residual * factor_second**3 * jnp.mean(
        residual * weighted, axis=-1, keepdims=True
    )
    grad_gain_mlp = jnp.sum(grad_mlp_input * residual * factor_second, axis=0)
    grad_attn = (grad_residual + scaled_grad).astype(bf16)
    grad_mixed = lax.dot_general(
        grad_attn, w_out, (((1,), (1,)), ((), ())), preferred_element_type=f32
    ).astype(bf16)
    grad_heads = heads(grad_mixed)
    grad_probs = jnp.einsum("qhe,khe->hqk", grad_heads, values, preferred_element_type=f32)
    inner_sum = jnp.sum(probs * grad_probs, axis=-1, keepdims=True)
    grad_raw = (probs * (grad_probs - inner_sum) * scaling).astype(bf16)

    def flat(products):
        return products.reshape(routed_len, -1).astype(bf16)

    grad_query = flat(jnp.einsum("hqk,khe->qhe", grad_raw, keys, preferred_element_type=f32))
    grad_key = flat(jnp.einsum("hqk,qhe->khe", grad_raw, queries, preferred_element_type=f32))
    grad_value = flat(jnp.einsum("hqk,qhe->khe", probs_low, grad_heads, preferred_element_type=f32))
    grad_parts = (grad_query, grad_key, grad_value)
    grad_attn_input = tp_sum(
        sum(
            lax.dot_general(
                grad_parts[c], weights[c], (((1,), (1,)), ((), ())), preferred_element_type=f32
            )
            for c in range(3)
        ),
        core,
    )
    grad_rows_flat = jnp.concatenate(grad_parts, axis=1)
    attn_pairs = jnp.concatenate(
        [outer(attn_input, grad_rows_flat), outer(grad_attn, mixed)], axis=1
    )
    attn_grads = ring_scatter(attn_pairs, 0, core)
    split = 3 * mixed.shape[1]
    grad_qkv = attn_grads[:, :split].reshape(-1, 3, mixed.shape[1])
    grad_out = attn_grads[:, split:].T

    branch = attn_out + mlp_out
    update = (gating * branch).astype(bf16)
    grad_score = gating * (1.0 - gating) * jnp.sum(grad_rows * branch, axis=-1, keepdims=True)
    weighted = grad_attn_input * gain_first
    grad_norm = factor_first * weighted - rows * factor_first**3 * jnp.mean(
        rows * weighted, axis=-1, keepdims=True
    )
    grad_gain_attn = jnp.sum(grad_attn_input * rows * factor_first, axis=0)
    grad_router = jnp.sum(grad_score * rows, axis=0)
    grad_routed_in = (grad_residual + grad_norm + grad_score * router).astype(bf16)

    small = jnp.stack([grad_gain_attn, grad_gain_mlp, grad_router]).astype(bf16)
    small = small.reshape(3, dev_count, -1).transpose(1, 0, 2)
    small = jnp.pad(small, ((0, 0), (0, 13), (0, half_width - small.shape[2])))
    sent = to_owners(pick_half(update, core), share)
    got_update = lax.all_to_all(sent, "seq", 0, 0, tiled=True)
    sent = jnp.concatenate([to_owners(pick_half(grad_routed_in, core), share), small], axis=1)
    got = lax.all_to_all(sent, "seq", 0, 0, tiled=True)
    small = jnp.sum(got[:, 2 * share : 2 * share + 3, : model_width // dev_count].astype(f32), axis=0)
    got_grad = got[:, : 2 * share]
    block_rows = join_halves(got_update, tp_permute(got_update, 1), core)
    grad_slots = join_halves(got_grad, tp_permute(got_grad, 1), core)
    block_out = (tokens.astype(f32) + spread(table, block_rows)).astype(bf16)
    grad_tokens = out_grad.astype(f32) + spread(table, grad_slots)
    return (
        block_out,
        grad_tokens,
        small[0],
        grad_qkv,
        grad_out,
        small[1],
        grad_up,
        grad_down,
        small[2],
    )


def solution(mesh):
    def on_device(*arrays):
        seq_count, routed_len = arrays[2].shape
        dev_count = mesh.shape["seq"]
        whole = seq_count == dev_count and mesh.shape["tp"] == 4 and dev_count % 2 == 0
        body = on_device_whole if whole else on_device_split
        return body(*arrays)

    return jax.shard_map(
        on_device,
        mesh=mesh,
        in_specs=(
            P(None, "seq", None),
            P(),
            P(),
            P(),
            P(None, None, "tp"),
            P("tp", None),
            P(),
            P(None, "tp"),
            P("tp", None),
            P(),
            P(None, "seq", None),
        ),
        out_specs=(
            P(None, "seq", None),
            P(None, "seq", None),
            P("seq"),
            P("seq", None, "tp"),
            P("tp", "seq"),
            P("seq"),
            P("seq", "tp"),
            P("tp", "seq"),
            P("seq"),
        ),
        check_vma=False,
    )
```

```python
import jax
import jax.numpy as jnp
from jax import lax
from jax.sharding import PartitionSpec as P

HEAD_DIM = 64


precise = lax.Precision.HIGHEST


def normed(values, gain):
    factor = lax.rsqrt(jnp.mean(values * values, axis=-1, keepdims=True) + 1e-05)
    return values * factor * gain


def gelu_tanh(values):
    return jax.nn.gelu(values, approximate=True)


def match_table(positions, usable, anchor, extent):
    offsets = jnp.arange(extent, dtype=jnp.int32)
    hits = (positions - anchor)[:, :, None] == offsets[None, None, :]
    return jnp.logical_and(hits, usable[:, :, None]).astype(jnp.bfloat16)


def compact(table, source):
    return jnp.einsum("sqc,scd->sqd", table, source, preferred_element_type=jnp.float32)


def spread(table, routed_rows):
    return jnp.einsum("sqc,sqd->scd", table, routed_rows, preferred_element_type=jnp.float32)


def on_device_split(
    tokens,
    seg_ids,
    routed_index,
    gain_attn,
    w_qkv,
    w_out,
    gain_mlp,
    w_up,
    w_down,
    w_router,
    out_grad,
):
    seq_count, group_len, model_width = tokens.shape
    routed_len = routed_index.shape[1]
    dev_count = lax.axis_size("seq")
    dev_index = lax.axis_index("seq")
    per_dev = routed_len // dev_count
    group_base = dev_index * group_len
    seg_routed = jnp.take_along_axis(seg_ids, routed_index, axis=1)
    capacity = 2 * per_dev
    slot_ids = jnp.arange(capacity, dtype=jnp.int32)
    first_rank = jnp.sum((routed_index < group_base).astype(jnp.int32), axis=1)
    group_count = (
        jnp.sum((routed_index < group_base + group_len).astype(jnp.int32), axis=1) - first_rank
    )
    query_rank = first_rank[:, None] + slot_ids[None, :]
    query_valid = slot_ids[None, :] < group_count[:, None]
    clipped = jnp.minimum(query_rank, routed_len - 1)
    query_pos = jnp.take_along_axis(routed_index, clipped, axis=1)
    own_table = match_table(query_pos, query_valid, group_base, group_len)
    routed_rows = compact(own_table, tokens).astype(jnp.bfloat16)
    routed_grads = compact(own_table, out_grad).astype(jnp.bfloat16)
    query_seg = jnp.take_along_axis(seg_routed, clipped, axis=1)
    bounds = jnp.arange(dev_count, dtype=jnp.int32) * group_len
    firsts = jnp.sum((routed_index[:, :, None] < bounds[None, None, :]).astype(jnp.int32), axis=1)
    next_firsts = jnp.concatenate(
        [firsts[:, 1:], jnp.full((seq_count, 1), routed_len, jnp.int32)], axis=1
    )
    key_rank = (firsts[:, :, None] + slot_ids[None, None, :]).reshape(seq_count, -1)
    key_valid = (slot_ids[None, None, :] < (next_firsts - firsts)[:, :, None]).reshape(
        seq_count, -1
    )
    key_seg = jnp.take_along_axis(seg_routed, jnp.minimum(key_rank, routed_len - 1), axis=1)
    allowed = jnp.logical_and(
        key_rank[:, None, :] <= query_rank[:, :, None], key_seg[:, None, :] == query_seg[:, :, None]
    )
    allowed = jnp.logical_and(allowed, key_valid[:, None, :])[:, None]
    rows_float = routed_rows.astype(jnp.float32)
    gain_first = gain_attn.astype(jnp.float32)
    gain_second = gain_mlp.astype(jnp.float32)
    router_score = jnp.einsum(
        "sqd,d->sq", routed_rows, w_router, preferred_element_type=jnp.float32
    )
    gating = jax.nn.sigmoid(router_score)
    attn_input = normed(rows_float, gain_first).astype(jnp.bfloat16)
    qkv_rows = jnp.einsum(
        "sqd,dch->sqch", attn_input, w_qkv, preferred_element_type=jnp.float32
    ).astype(jnp.bfloat16)
    query_count = qkv_rows.shape[1]
    head_count = qkv_rows.shape[3] // HEAD_DIM
    query_flat = qkv_rows[:, :, 0]
    queries = query_flat.reshape(seq_count, query_count, head_count, HEAD_DIM)
    key_pair = (qkv_rows[:, :, 1], qkv_rows[:, :, 2])
    all_keys = lax.all_gather(key_pair[0], "seq", axis=1, tiled=True)
    all_values = lax.all_gather(key_pair[1], "seq", axis=1, tiled=True)
    key_count = all_keys.shape[1]
    all_keys = all_keys.reshape(seq_count, key_count, head_count, HEAD_DIM)
    all_values = all_values.reshape(seq_count, key_count, head_count, HEAD_DIM)
    scaling = HEAD_DIM ** (-0.5)

    def masked_logits():
        raw_scores = jnp.einsum(
            "sqhe,skhe->shqk", queries, all_keys, preferred_element_type=jnp.float32
        )
        return jnp.where(allowed, raw_scores * scaling, -1e30)

    logits = masked_logits()
    row_peak = jnp.max(logits, axis=-1, keepdims=True)
    powered = jnp.exp(logits - row_peak)
    row_total = jnp.sum(powered, axis=-1, keepdims=True)
    log_total = row_peak + jnp.log(row_total)
    probs_low = (powered / row_total).astype(jnp.bfloat16)
    mixed = jnp.einsum("shqk,skhe->sqhe", probs_low, all_values, preferred_element_type=jnp.float32)
    mixed = mixed.reshape(seq_count, query_count, -1).astype(jnp.bfloat16)
    attn_out = lax.psum(
        jnp.einsum("sqh,hd->sqd", mixed, w_out, preferred_element_type=jnp.float32).astype(
            jnp.bfloat16
        ),
        "tp",
    ).astype(jnp.float32)
    residual = rows_float + attn_out
    mlp_input = normed(residual, gain_second).astype(jnp.bfloat16)
    pre_act = jnp.einsum("sqd,df->sqf", mlp_input, w_up, preferred_element_type=jnp.float32)
    hidden = gelu_tanh(pre_act).astype(jnp.bfloat16)
    mlp_out = lax.psum(
        jnp.einsum("sqf,fd->sqd", hidden, w_down, preferred_element_type=jnp.float32).astype(
            jnp.bfloat16
        ),
        "tp",
    ).astype(jnp.float32)
    branch = attn_out + mlp_out
    update_rows = (gating[:, :, None] * branch).astype(jnp.bfloat16)
    block_out = (tokens.astype(jnp.float32) + spread(own_table, update_rows)).astype(jnp.bfloat16)
    grad_rows = routed_grads.astype(jnp.float32)
    scaled_grad = gating[:, :, None] * grad_rows
    grad_score = jnp.sum(grad_rows * branch, axis=-1) * gating * (1.0 - gating)
    grad_mlp = scaled_grad.astype(jnp.bfloat16)
    grad_down = jnp.einsum("sqf,sqd->fd", hidden, grad_mlp, preferred_element_type=jnp.float32)
    grad_hidden = jnp.einsum("sqd,fd->sqf", grad_mlp, w_down, preferred_element_type=jnp.float32)
    gelu_pull = jax.vjp(gelu_tanh, pre_act)[1]
    grad_pre = gelu_pull(grad_hidden)[0].astype(jnp.bfloat16)
    grad_up = jnp.einsum("sqd,sqf->df", mlp_input, grad_pre, preferred_element_type=jnp.float32)
    grad_mlp_input = lax.psum(
        jnp.einsum("sqf,df->sqd", grad_pre, w_up, preferred_element_type=jnp.float32).astype(
            jnp.bfloat16
        ),
        "tp",
    ).astype(jnp.float32)
    second_pull = jax.vjp(normed, residual, gain_second)[1]
    grad_residual, grad_gain_mlp = second_pull(grad_mlp_input)
    grad_attn = (grad_residual + scaled_grad).astype(jnp.bfloat16)
    grad_out = jnp.einsum("sqh,sqd->hd", mixed, grad_attn, preferred_element_type=jnp.float32)
    grad_mixed_flat = jnp.einsum(
        "sqd,hd->sqh", grad_attn, w_out, preferred_element_type=jnp.float32
    ).astype(jnp.bfloat16)
    grad_mixed = grad_mixed_flat.reshape(seq_count, query_count, head_count, HEAD_DIM)
    probs_again = jnp.where(allowed, jnp.exp(masked_logits() - log_total), 0.0)
    grad_probs = jnp.einsum(
        "sqhe,skhe->shqk", grad_mixed, all_values, preferred_element_type=jnp.float32
    )
    inner_sum = jnp.sum(probs_again * grad_probs, axis=-1, keepdims=True)
    grad_raw = (probs_again * (grad_probs - inner_sum) * scaling).astype(jnp.bfloat16)
    grad_query = jnp.einsum(
        "shqk,skhe->sqhe", grad_raw, all_keys, preferred_element_type=jnp.float32
    )
    grad_query = grad_query.reshape(seq_count, query_count, -1).astype(jnp.bfloat16)
    probs_again_low = probs_again.astype(jnp.bfloat16)
    key_part = jnp.einsum(
        "shqk,sqhe->skhe", grad_raw, queries, preferred_element_type=jnp.float32
    ).reshape(seq_count, key_count, -1)
    value_part = jnp.einsum(
        "shqk,sqhe->skhe", probs_again_low, grad_mixed, preferred_element_type=jnp.float32
    ).reshape(seq_count, key_count, -1)
    key_pair = (key_part, value_part)
    grad_keys = lax.psum_scatter(key_pair[0], "seq", scatter_dimension=1, tiled=True)
    grad_values = lax.psum_scatter(key_pair[1], "seq", scatter_dimension=1, tiled=True)
    grad_qkv_rows = jnp.stack(
        [grad_query, grad_keys.astype(jnp.bfloat16), grad_values.astype(jnp.bfloat16)], axis=2
    )
    grad_qkv = jnp.einsum(
        "sqd,sqch->dch", attn_input, grad_qkv_rows, preferred_element_type=jnp.float32
    )
    grad_attn_input = lax.psum(
        jnp.einsum(
            "sqch,dch->sqd", grad_qkv_rows, w_qkv, preferred_element_type=jnp.float32
        ).astype(jnp.bfloat16),
        "tp",
    ).astype(jnp.float32)
    first_pull = jax.vjp(normed, rows_float, gain_first)[1]
    grad_norm, grad_gain_attn = first_pull(grad_attn_input)
    grad_router = jnp.einsum("sq,sqd->d", grad_score, rows_float, precision=precise)
    grad_routed_in = (
        grad_residual + grad_norm + grad_score[:, :, None] * w_router.astype(jnp.float32)
    ).astype(jnp.bfloat16)
    grad_tokens = out_grad.astype(jnp.float32) + spread(own_table, grad_routed_in)
    reduced = (
        lax.psum_scatter(grad_gain_attn, "seq", scatter_dimension=0, tiled=True),
        lax.psum_scatter(grad_qkv, "seq", scatter_dimension=0, tiled=True),
        lax.psum_scatter(grad_out, "seq", scatter_dimension=1, tiled=True),
        lax.psum_scatter(grad_gain_mlp, "seq", scatter_dimension=0, tiled=True),
        lax.psum_scatter(grad_up, "seq", scatter_dimension=0, tiled=True),
        lax.psum_scatter(grad_down, "seq", scatter_dimension=1, tiled=True),
        lax.psum_scatter(grad_router, "seq", scatter_dimension=0, tiled=True),
    )
    return (block_out, grad_tokens) + tuple(reduced)


def ring_order(size):
    return list(range(0, size, 2)) + list(range(size - 1, 0, -2))


def ring_place(index, size):
    return jnp.where(index % 2 == 0, index // 2, size - 1 - index // 2)


def ring_owner(place, size):
    place = place % size
    return jnp.where(place < size // 2, 2 * place, 2 * (size - place) - 1)


def ring_permute(values, sign):
    order = ring_order(lax.axis_size("seq"))
    size, width = len(order), lax.axis_size("tp")
    pairs = []
    for i in range(size):
        for t in range(width):
            there = (i + sign * (1 - 2 * (t % 2))) % size
            pairs.append((order[i] * width + t, order[there] * width + t))
    return lax.ppermute(values, ("seq", "tp"), pairs)


def after(value, *others):
    return lax.optimization_barrier((value,) + others)[0]


def ring_chunk(whole, axis, core, distance):
    size = lax.axis_size("seq")
    place = ring_place(lax.axis_index("seq"), size)
    width = whole.shape[axis] // size
    owner = ring_owner(place + size + distance * (1 - 2 * core), size)
    return lax.dynamic_slice_in_dim(whole, owner * width, width, axis)


def ring_step(whole, axis, core, state, step, *others):
    size = lax.axis_size("seq")
    far, near = size // 2, size // 2 - 1
    f32, bf16 = jnp.float32, jnp.bfloat16

    def chunk(distance):
        return ring_chunk(whole, axis, core, distance)

    if step == 0:
        return chunk(far), chunk(-near)
    ahead = after(ring_permute(state[0], 1), *others)
    if step == far:
        return chunk(0).astype(f32) + ahead.astype(f32) + state[1].astype(f32)
    behind = after(ring_permute(state[1], -1), *others)
    ahead = (ahead.astype(f32) + chunk(far - step).astype(f32)).astype(bf16)
    if step < near:
        behind = (behind.astype(f32) + chunk(step - near).astype(f32)).astype(bf16)
    return ahead, behind


def tp_permute(values, mask):
    size = lax.axis_size("tp")
    return lax.ppermute(values, "tp", [(i, i ^ mask) for i in range(size)])


def pick_half(values, which):
    width = values.shape[-1] // 2
    return jnp.where(which == 0, values[..., :width], values[..., width:])


def join_halves(own, other, which):
    return jnp.where(
        which == 0,
        jnp.concatenate([own, other], axis=-1),
        jnp.concatenate([other, own], axis=-1),
    )


def tp_start(partial, which):
    narrow = partial.astype(jnp.bfloat16)
    moved = tp_permute(pick_half(narrow, 1 - which), 1)
    half = pick_half(partial, which) + moved.astype(jnp.float32)
    return half.astype(jnp.bfloat16)


def tp_cross(half, *others):
    moved = after(tp_permute(half, 2), *others)
    return (half.astype(jnp.float32) + moved.astype(jnp.float32)).astype(jnp.bfloat16)


def tp_join(half, which):
    return join_halves(half, tp_permute(half, 1), which).astype(jnp.float32)


def to_owners(rows, share):
    groups = rows.reshape(-1, share, rows.shape[-1])
    later = jnp.concatenate([groups[1:], jnp.zeros_like(groups[:1])], axis=0)
    return jnp.concatenate([groups, later], axis=1)


def from_owners(slots, share):
    later = jnp.concatenate([jnp.zeros_like(slots[:1, share:]), slots[:-1, share:]], axis=0)
    return (slots[:, :share] + later).reshape(-1, slots.shape[-1])


def on_device_whole(
    tokens,
    seg_ids,
    routed_index,
    gain_attn,
    w_qkv,
    w_out,
    gain_mlp,
    w_up,
    w_down,
    w_router,
    out_grad,
):
    f32, bf16 = jnp.float32, jnp.bfloat16
    seq_count, group_len, model_width = tokens.shape
    routed_len = routed_index.shape[1]
    dev_count = lax.axis_size("seq")
    dev_index = lax.axis_index("seq")
    core = lax.axis_index("tp") % 2
    side = lax.axis_index("tp") // 2
    share = routed_len // dev_count
    half_width = model_width // 2

    padded_index = jnp.concatenate(
        [routed_index, jnp.full((seq_count, share), -1, jnp.int32)], axis=1
    )
    slots = lax.dynamic_slice(padded_index, (0, dev_index * share), (seq_count, 2 * share))
    offsets = jnp.arange(group_len, dtype=jnp.int32)
    table = ((slots - dev_index * group_len)[:, :, None] == offsets).astype(bf16)

    index_row = lax.dynamic_index_in_dim(routed_index, dev_index, 0, False)
    seg_row = lax.dynamic_index_in_dim(seg_ids, dev_index, 0, False)
    seg_routed = sum(
        (index_row >= jnp.sum((seg_row < t).astype(jnp.int32))).astype(jnp.int32)
        for t in range(1, 4)
    )
    def pick(source):
        own = lax.dynamic_slice_in_dim(source, core * half_width, half_width, 2)
        return compact(table, own).astype(bf16)

    def exchange(own):
        return lax.all_to_all(own, "seq", 0, 0, tiled=True)

    def settle(slots):
        own = from_owners(slots, share)
        return join_halves(own, tp_permute(own, 1), core)

    slots, seg_routed, picked_grads = lax.optimization_barrier(
        (exchange(pick(tokens)), seg_routed, pick(out_grad))
    )
    routed_rows = settle(slots)

    ranks = jnp.arange(routed_len, dtype=jnp.int32)
    allowed = jnp.logical_and(
        ranks[None, :] <= ranks[:, None], seg_routed[None, :] == seg_routed[:, None]
    )[None]

    rows = routed_rows.astype(f32)
    gain_first = gain_attn.astype(f32)
    gain_second = gain_mlp.astype(f32)
    router = w_router.astype(f32)
    gating = jax.nn.sigmoid(jnp.sum(rows * router, axis=-1, keepdims=True))
    factor_first = lax.rsqrt(jnp.mean(rows * rows, axis=-1, keepdims=True) + 1e-05)
    attn_input = (rows * factor_first * gain_first).astype(bf16)
    weights = jnp.transpose(w_qkv, (1, 0, 2))
    qkv = jnp.einsum("rd,cdh->crh", attn_input, weights, preferred_element_type=f32).astype(bf16)
    head_count = qkv.shape[2] // HEAD_DIM
    scaling = HEAD_DIM ** (-0.5)

    def heads(values):
        return values.reshape(routed_len, head_count, HEAD_DIM)

    queries, keys, values = heads(qkv[0]), heads(qkv[1]), heads(qkv[2])
    raw = jnp.einsum("qhe,khe->hqk", queries, keys, preferred_element_type=f32)
    logits = jnp.where(allowed, raw * scaling, -1e30)
    powered = jnp.exp(logits - jnp.max(logits, axis=-1, keepdims=True))
    probs = powered / jnp.sum(powered, axis=-1, keepdims=True)
    probs_low = probs.astype(bf16)
    mixed = jnp.einsum("hqk,khe->qhe", probs_low, values, preferred_element_type=f32)
    mixed = mixed.reshape(routed_len, -1).astype(bf16)
    mixed, grad_slots = lax.optimization_barrier((mixed, exchange(picked_grads)))
    attn_half = tp_start(jnp.dot(mixed, w_out, preferred_element_type=f32), core)
    grad_rows = settle(grad_slots).astype(f32)
    attn_half = tp_cross(attn_half)
    attn_out = tp_join(attn_half, core)

    residual = rows + attn_out
    factor_second = lax.rsqrt(jnp.mean(residual * residual, axis=-1, keepdims=True) + 1e-05)
    mlp_input = (residual * factor_second * gain_second).astype(bf16)
    scaled_grad = gating * grad_rows
    grad_mlp = scaled_grad.astype(bf16)
    pre_act = jnp.dot(mlp_input, w_up, preferred_element_type=f32)
    hidden, gelu_pull = jax.vjp(gelu_tanh, pre_act)
    hidden = hidden.astype(bf16)
    grad_hidden = lax.dot_general(
        grad_mlp, w_down, (((1,), (1,)), ((), ())), preferred_element_type=f32
    )
    grad_pre = gelu_pull(grad_hidden)[0].astype(bf16)
    pull_part = lax.dot_general(
        grad_pre, w_up, (((1,), (1,)), ((), ())), preferred_element_type=f32
    )
    pull_half = tp_start(pull_part, core)
    mlp_half = tp_start(
        jnp.dot(after(hidden, pull_half), w_down, preferred_element_type=f32), core
    )

    def outer(left, right):
        product = lax.dot_general(
            left, right, (((0,), (0,)), ((), ())), preferred_element_type=f32
        )
        return product.astype(bf16)

    mlp_pairs = lax.dot_general(
        jnp.stack([mlp_input, grad_mlp]),
        jnp.stack([grad_pre, hidden]),
        (((1,), (1,)), ((0,), (0,))),
        preferred_element_type=f32,
    ).astype(bf16)

    def mlp_ring(total, step, *others):
        return ring_step(mlp_pairs, 1, core, total, step, *others)

    mlp_ring_0 = mlp_ring(None, 0)
    mlp_ring_1 = mlp_ring(mlp_ring_0, 1)
    pull_half, mlp_half = lax.optimization_barrier(
        (tp_cross(pull_half, *mlp_ring_1, mlp_half), mlp_half)
    )
    quarter = pick_half(attn_half, side).astype(f32) + pick_half(mlp_half, side).astype(f32)
    branch_part = quarter + tp_permute(pick_half(mlp_half, 1 - side), 2).astype(f32)
    grad_mlp_input = tp_join(pull_half, core)

    weighted = grad_mlp_input * gain_second
    grad_residual = factor_second * weighted - residual * factor_second**3 * jnp.mean(
        residual * weighted, axis=-1, keepdims=True
    )
    grad_gain_mlp = jnp.sum(grad_mlp_input * residual * factor_second, axis=0)
    grad_attn = (grad_residual + scaled_grad).astype(bf16)
    grad_mixed = lax.dot_general(
        grad_attn, w_out, (((1,), (1,)), ((), ())), preferred_element_type=f32
    ).astype(bf16)
    grad_heads = heads(grad_mixed)
    grad_probs = jnp.einsum("qhe,khe->hqk", grad_heads, values, preferred_element_type=f32)
    inner_sum = jnp.sum(probs * grad_probs, axis=-1, keepdims=True)
    grad_raw = (probs * (grad_probs - inner_sum) * scaling).astype(bf16)
    def flat(products):
        return products.reshape(routed_len, -1).astype(bf16)

    grad_query = flat(jnp.einsum("hqk,khe->qhe", grad_raw, keys, preferred_element_type=f32))
    grad_key = flat(jnp.einsum("hqk,qhe->khe", grad_raw, queries, preferred_element_type=f32))
    grad_value = flat(jnp.einsum("hqk,qhe->khe", probs_low, grad_heads, preferred_element_type=f32))
    mlp_ring_2 = mlp_ring(mlp_ring_1, 2)
    grad_query, grad_key, grad_value, branch_part, mlp_ring_2 = lax.optimization_barrier(
        (grad_query, grad_key, grad_value, branch_part, mlp_ring_2)
    )
    grad_parts = (grad_query, grad_key, grad_value)
    update = (gating * branch_part).astype(bf16)
    score = jnp.sum(pick_half(pick_half(grad_rows, core), side) * branch_part, axis=-1)
    score = score + tp_permute(score, 1)
    score = score + tp_permute(score, 2)
    down_part = sum(
        lax.dot_general(
            grad_parts[c], weights[c], (((1,), (1,)), ((), ())), preferred_element_type=f32
        )
        for c in range(3)
    )
    input_half = tp_start(down_part, core)

    grad_rows_flat = jnp.concatenate(grad_parts, axis=1)
    attn_pairs = jnp.concatenate(
        [outer(attn_input, grad_rows_flat), outer(grad_attn, mixed)], axis=1
    )

    def attn_ring(total, step, *others):
        return ring_step(attn_pairs, 0, core, total, step, *others)

    attn_ring_0 = attn_ring(None, 0)

    input_half, score = lax.optimization_barrier((tp_cross(input_half), score))
    grad_score = gating * (1.0 - gating) * score[:, None]
    grad_attn_input = tp_join(input_half, core)
    weighted = grad_attn_input * gain_first
    grad_norm = factor_first * weighted - rows * factor_first**3 * jnp.mean(
        rows * weighted, axis=-1, keepdims=True
    )
    grad_gain_attn = jnp.sum(grad_attn_input * rows * factor_first, axis=0)
    grad_router = jnp.sum(grad_score * rows, axis=0)
    grad_routed_in = (grad_residual + grad_norm + grad_score * router).astype(bf16)

    small = jnp.stack([grad_gain_attn, grad_gain_mlp, grad_router]).astype(bf16)
    small = small.reshape(3, dev_count, -1).transpose(1, 0, 2)
    small = jnp.pad(small, ((0, 0), (0, 13), (0, half_width - small.shape[2])))
    grads_part = pick_half(pick_half(grad_routed_in, core), side)
    pieces = to_owners(jnp.concatenate([update, grads_part], axis=1), share)
    sent = jnp.concatenate([pieces, small], axis=1)
    got = lax.all_to_all(sent, "seq", 0, 0, tiled=True)
    mlp_total = mlp_ring(mlp_ring_2, 3, sent)
    attn_total = attn_ring(attn_ring_0, 1, sent)
    for step in range(4, dev_count // 2 + 1):
        mlp_total = mlp_ring(mlp_total, step)
    for step in range(2, dev_count // 2 + 1):
        if step == 3:
            attn_total, got = lax.optimization_barrier((attn_total, got))
        attn_total = attn_ring(attn_total, step)
    grad_up, grad_down = mlp_total[0], mlp_total[1].T
    split = 3 * mixed.shape[1]
    grad_qkv = attn_total[:, :split].reshape(-1, 3, mixed.shape[1])
    grad_out = attn_total[:, split:].T

    small = jnp.sum(got[:, 2 * share : 2 * share + 3, : model_width // dev_count].astype(f32), axis=0)
    width = half_width // 2

    def gather(part):
        part = join_halves(part, tp_permute(part, 2), side)
        return join_halves(part, tp_permute(part, 1), core)

    block_rows = gather(got[:, : 2 * share, :width])
    grad_slots = gather(got[:, : 2 * share, width:])
    block_out = (tokens.astype(f32) + spread(table, block_rows)).astype(bf16)
    grad_tokens = out_grad.astype(f32) + spread(table, grad_slots)
    return (
        block_out,
        grad_tokens,
        small[0],
        grad_qkv,
        grad_out,
        small[1],
        grad_up,
        grad_down,
        small[2],
    )


def solution(mesh):
    def on_device(*arrays):
        seq_count, routed_len = arrays[2].shape
        dev_count = mesh.shape["seq"]
        whole = seq_count == dev_count and mesh.shape["tp"] == 4 and dev_count % 2 == 0
        body = on_device_whole if whole else on_device_split
        return body(*arrays)

    return jax.shard_map(
        on_device,
        mesh=mesh,
        in_specs=(
            P(None, "seq", None),
            P(),
            P(),
            P(),
            P(None, None, "tp"),
            P("tp", None),
            P(),
            P(None, "tp"),
            P("tp", None),
            P(),
            P(None, "seq", None),
        ),
        out_specs=(
            P(None, "seq", None),
            P(None, "seq", None),
            P("seq"),
            P("seq", None, "tp"),
            P("tp", "seq"),
            P("seq"),
            P("seq", "tp"),
            P("tp", "seq"),
            P("seq"),
        ),
        check_vma=False,
    )
```

```python
import jax
import jax.numpy as jnp
from jax import lax
from jax.sharding import PartitionSpec as P

HEAD_DIM = 64


precise = lax.Precision.HIGHEST


def normed(values, gain):
    factor = lax.rsqrt(jnp.mean(values * values, axis=-1, keepdims=True) + 1e-05)
    return values * factor * gain


def gelu_tanh(values):
    return jax.nn.gelu(values, approximate=True)


def match_table(positions, usable, anchor, extent):
    offsets = jnp.arange(extent, dtype=jnp.int32)
    hits = (positions - anchor)[:, :, None] == offsets[None, None, :]
    return jnp.logical_and(hits, usable[:, :, None]).astype(jnp.bfloat16)


def compact(table, source):
    return jnp.einsum("sqc,scd->sqd", table, source, preferred_element_type=jnp.float32)


def spread(table, routed_rows):
    return jnp.einsum("sqc,sqd->scd", table, routed_rows, preferred_element_type=jnp.float32)


def on_device_split(
    tokens,
    seg_ids,
    routed_index,
    gain_attn,
    w_qkv,
    w_out,
    gain_mlp,
    w_up,
    w_down,
    w_router,
    out_grad,
):
    seq_count, group_len, model_width = tokens.shape
    routed_len = routed_index.shape[1]
    dev_count = lax.axis_size("seq")
    dev_index = lax.axis_index("seq")
    per_dev = routed_len // dev_count
    group_base = dev_index * group_len
    seg_routed = jnp.take_along_axis(seg_ids, routed_index, axis=1)
    capacity = 2 * per_dev
    slot_ids = jnp.arange(capacity, dtype=jnp.int32)
    first_rank = jnp.sum((routed_index < group_base).astype(jnp.int32), axis=1)
    group_count = (
        jnp.sum((routed_index < group_base + group_len).astype(jnp.int32), axis=1) - first_rank
    )
    query_rank = first_rank[:, None] + slot_ids[None, :]
    query_valid = slot_ids[None, :] < group_count[:, None]
    clipped = jnp.minimum(query_rank, routed_len - 1)
    query_pos = jnp.take_along_axis(routed_index, clipped, axis=1)
    own_table = match_table(query_pos, query_valid, group_base, group_len)
    routed_rows = compact(own_table, tokens).astype(jnp.bfloat16)
    routed_grads = compact(own_table, out_grad).astype(jnp.bfloat16)
    query_seg = jnp.take_along_axis(seg_routed, clipped, axis=1)
    bounds = jnp.arange(dev_count, dtype=jnp.int32) * group_len
    firsts = jnp.sum((routed_index[:, :, None] < bounds[None, None, :]).astype(jnp.int32), axis=1)
    next_firsts = jnp.concatenate(
        [firsts[:, 1:], jnp.full((seq_count, 1), routed_len, jnp.int32)], axis=1
    )
    key_rank = (firsts[:, :, None] + slot_ids[None, None, :]).reshape(seq_count, -1)
    key_valid = (slot_ids[None, None, :] < (next_firsts - firsts)[:, :, None]).reshape(
        seq_count, -1
    )
    key_seg = jnp.take_along_axis(seg_routed, jnp.minimum(key_rank, routed_len - 1), axis=1)
    allowed = jnp.logical_and(
        key_rank[:, None, :] <= query_rank[:, :, None], key_seg[:, None, :] == query_seg[:, :, None]
    )
    allowed = jnp.logical_and(allowed, key_valid[:, None, :])[:, None]
    rows_float = routed_rows.astype(jnp.float32)
    gain_first = gain_attn.astype(jnp.float32)
    gain_second = gain_mlp.astype(jnp.float32)
    router_score = jnp.einsum(
        "sqd,d->sq", routed_rows, w_router, preferred_element_type=jnp.float32
    )
    gating = jax.nn.sigmoid(router_score)
    attn_input = normed(rows_float, gain_first).astype(jnp.bfloat16)
    qkv_rows = jnp.einsum(
        "sqd,dch->sqch", attn_input, w_qkv, preferred_element_type=jnp.float32
    ).astype(jnp.bfloat16)
    query_count = qkv_rows.shape[1]
    head_count = qkv_rows.shape[3] // HEAD_DIM
    query_flat = qkv_rows[:, :, 0]
    queries = query_flat.reshape(seq_count, query_count, head_count, HEAD_DIM)
    key_pair = (qkv_rows[:, :, 1], qkv_rows[:, :, 2])
    all_keys = lax.all_gather(key_pair[0], "seq", axis=1, tiled=True)
    all_values = lax.all_gather(key_pair[1], "seq", axis=1, tiled=True)
    key_count = all_keys.shape[1]
    all_keys = all_keys.reshape(seq_count, key_count, head_count, HEAD_DIM)
    all_values = all_values.reshape(seq_count, key_count, head_count, HEAD_DIM)
    scaling = HEAD_DIM ** (-0.5)

    def masked_logits():
        raw_scores = jnp.einsum(
            "sqhe,skhe->shqk", queries, all_keys, preferred_element_type=jnp.float32
        )
        return jnp.where(allowed, raw_scores * scaling, -1e30)

    logits = masked_logits()
    row_peak = jnp.max(logits, axis=-1, keepdims=True)
    powered = jnp.exp(logits - row_peak)
    row_total = jnp.sum(powered, axis=-1, keepdims=True)
    log_total = row_peak + jnp.log(row_total)
    probs_low = (powered / row_total).astype(jnp.bfloat16)
    mixed = jnp.einsum("shqk,skhe->sqhe", probs_low, all_values, preferred_element_type=jnp.float32)
    mixed = mixed.reshape(seq_count, query_count, -1).astype(jnp.bfloat16)
    attn_out = lax.psum(
        jnp.einsum("sqh,hd->sqd", mixed, w_out, preferred_element_type=jnp.float32).astype(
            jnp.bfloat16
        ),
        "tp",
    ).astype(jnp.float32)
    residual = rows_float + attn_out
    mlp_input = normed(residual, gain_second).astype(jnp.bfloat16)
    pre_act = jnp.einsum("sqd,df->sqf", mlp_input, w_up, preferred_element_type=jnp.float32)
    hidden = gelu_tanh(pre_act).astype(jnp.bfloat16)
    mlp_out = lax.psum(
        jnp.einsum("sqf,fd->sqd", hidden, w_down, preferred_element_type=jnp.float32).astype(
            jnp.bfloat16
        ),
        "tp",
    ).astype(jnp.float32)
    branch = attn_out + mlp_out
    update_rows = (gating[:, :, None] * branch).astype(jnp.bfloat16)
    block_out = (tokens.astype(jnp.float32) + spread(own_table, update_rows)).astype(jnp.bfloat16)
    grad_rows = routed_grads.astype(jnp.float32)
    scaled_grad = gating[:, :, None] * grad_rows
    grad_score = jnp.sum(grad_rows * branch, axis=-1) * gating * (1.0 - gating)
    grad_mlp = scaled_grad.astype(jnp.bfloat16)
    grad_down = jnp.einsum("sqf,sqd->fd", hidden, grad_mlp, preferred_element_type=jnp.float32)
    grad_hidden = jnp.einsum("sqd,fd->sqf", grad_mlp, w_down, preferred_element_type=jnp.float32)
    gelu_pull = jax.vjp(gelu_tanh, pre_act)[1]
    grad_pre = gelu_pull(grad_hidden)[0].astype(jnp.bfloat16)
    grad_up = jnp.einsum("sqd,sqf->df", mlp_input, grad_pre, preferred_element_type=jnp.float32)
    grad_mlp_input = lax.psum(
        jnp.einsum("sqf,df->sqd", grad_pre, w_up, preferred_element_type=jnp.float32).astype(
            jnp.bfloat16
        ),
        "tp",
    ).astype(jnp.float32)
    second_pull = jax.vjp(normed, residual, gain_second)[1]
    grad_residual, grad_gain_mlp = second_pull(grad_mlp_input)
    grad_attn = (grad_residual + scaled_grad).astype(jnp.bfloat16)
    grad_out = jnp.einsum("sqh,sqd->hd", mixed, grad_attn, preferred_element_type=jnp.float32)
    grad_mixed_flat = jnp.einsum(
        "sqd,hd->sqh", grad_attn, w_out, preferred_element_type=jnp.float32
    ).astype(jnp.bfloat16)
    grad_mixed = grad_mixed_flat.reshape(seq_count, query_count, head_count, HEAD_DIM)
    probs_again = jnp.where(allowed, jnp.exp(masked_logits() - log_total), 0.0)
    grad_probs = jnp.einsum(
        "sqhe,skhe->shqk", grad_mixed, all_values, preferred_element_type=jnp.float32
    )
    inner_sum = jnp.sum(probs_again * grad_probs, axis=-1, keepdims=True)
    grad_raw = (probs_again * (grad_probs - inner_sum) * scaling).astype(jnp.bfloat16)
    grad_query = jnp.einsum(
        "shqk,skhe->sqhe", grad_raw, all_keys, preferred_element_type=jnp.float32
    )
    grad_query = grad_query.reshape(seq_count, query_count, -1).astype(jnp.bfloat16)
    probs_again_low = probs_again.astype(jnp.bfloat16)
    key_part = jnp.einsum(
        "shqk,sqhe->skhe", grad_raw, queries, preferred_element_type=jnp.float32
    ).reshape(seq_count, key_count, -1)
    value_part = jnp.einsum(
        "shqk,sqhe->skhe", probs_again_low, grad_mixed, preferred_element_type=jnp.float32
    ).reshape(seq_count, key_count, -1)
    key_pair = (key_part, value_part)
    grad_keys = lax.psum_scatter(key_pair[0], "seq", scatter_dimension=1, tiled=True)
    grad_values = lax.psum_scatter(key_pair[1], "seq", scatter_dimension=1, tiled=True)
    grad_qkv_rows = jnp.stack(
        [grad_query, grad_keys.astype(jnp.bfloat16), grad_values.astype(jnp.bfloat16)], axis=2
    )
    grad_qkv = jnp.einsum(
        "sqd,sqch->dch", attn_input, grad_qkv_rows, preferred_element_type=jnp.float32
    )
    grad_attn_input = lax.psum(
        jnp.einsum(
            "sqch,dch->sqd", grad_qkv_rows, w_qkv, preferred_element_type=jnp.float32
        ).astype(jnp.bfloat16),
        "tp",
    ).astype(jnp.float32)
    first_pull = jax.vjp(normed, rows_float, gain_first)[1]
    grad_norm, grad_gain_attn = first_pull(grad_attn_input)
    grad_router = jnp.einsum("sq,sqd->d", grad_score, rows_float, precision=precise)
    grad_routed_in = (
        grad_residual + grad_norm + grad_score[:, :, None] * w_router.astype(jnp.float32)
    ).astype(jnp.bfloat16)
    grad_tokens = out_grad.astype(jnp.float32) + spread(own_table, grad_routed_in)
    reduced = (
        lax.psum_scatter(grad_gain_attn, "seq", scatter_dimension=0, tiled=True),
        lax.psum_scatter(grad_qkv, "seq", scatter_dimension=0, tiled=True),
        lax.psum_scatter(grad_out, "seq", scatter_dimension=1, tiled=True),
        lax.psum_scatter(grad_gain_mlp, "seq", scatter_dimension=0, tiled=True),
        lax.psum_scatter(grad_up, "seq", scatter_dimension=0, tiled=True),
        lax.psum_scatter(grad_down, "seq", scatter_dimension=1, tiled=True),
        lax.psum_scatter(grad_router, "seq", scatter_dimension=0, tiled=True),
    )
    return (block_out, grad_tokens) + tuple(reduced)


def ring_order(size):
    return list(range(0, size, 2)) + list(range(size - 1, 0, -2))


def ring_place(index, size):
    return jnp.where(index % 2 == 0, index // 2, size - 1 - index // 2)


def ring_owner(place, size):
    place = place % size
    return jnp.where(place < size // 2, 2 * place, 2 * (size - place) - 1)


def ring_permute(values, sign):
    order = ring_order(lax.axis_size("seq"))
    size, width = len(order), lax.axis_size("tp")
    pairs = []
    for i in range(size):
        for t in range(width):
            there = (i + sign * (1 - 2 * (t % 2))) % size
            pairs.append((order[i] * width + t, order[there] * width + t))
    return lax.ppermute(values, ("seq", "tp"), pairs)


def after(value, *others):
    return lax.optimization_barrier((value,) + others)[0]


def ring_chunk(whole, axis, core, distance):
    size = lax.axis_size("seq")
    place = ring_place(lax.axis_index("seq"), size)
    width = whole.shape[axis] // size
    owner = ring_owner(place + size + distance * (1 - 2 * core), size)
    return lax.dynamic_slice_in_dim(whole, owner * width, width, axis)


def ring_step(whole, axis, core, state, step, *others):
    size = lax.axis_size("seq")
    far, near = size // 2, size // 2 - 1
    f32, bf16 = jnp.float32, jnp.bfloat16

    def chunk(distance):
        return ring_chunk(whole, axis, core, distance)

    if step == 0:
        return chunk(far), chunk(-near)
    ahead = after(ring_permute(state[0], 1), *others)
    if step == far:
        return chunk(0).astype(f32) + ahead.astype(f32) + state[1].astype(f32)
    behind = after(ring_permute(state[1], -1), *others)
    ahead = (ahead.astype(f32) + chunk(far - step).astype(f32)).astype(bf16)
    if step < near:
        behind = (behind.astype(f32) + chunk(step - near).astype(f32)).astype(bf16)
    return ahead, behind


def tp_permute(values, mask):
    size = lax.axis_size("tp")
    return lax.ppermute(values, "tp", [(i, i ^ mask) for i in range(size)])


def pick_half(values, which):
    width = values.shape[-1] // 2
    return jnp.where(which == 0, values[..., :width], values[..., width:])


def join_halves(own, other, which):
    return jnp.where(
        which == 0,
        jnp.concatenate([own, other], axis=-1),
        jnp.concatenate([other, own], axis=-1),
    )


def tp_start(partial, which):
    narrow = partial.astype(jnp.bfloat16)
    moved = tp_permute(pick_half(narrow, 1 - which), 1)
    half = pick_half(partial, which) + moved.astype(jnp.float32)
    return half.astype(jnp.bfloat16)


def tp_cross(half, *others):
    moved = after(tp_permute(half, 2), *others)
    return (half.astype(jnp.float32) + moved.astype(jnp.float32)).astype(jnp.bfloat16)


def tp_join(half, which, *others):
    return join_halves(half, after(tp_permute(half, 1), *others), which).astype(jnp.float32)


def to_owners(rows, share):
    groups = rows.reshape(-1, share, rows.shape[-1])
    later = jnp.concatenate([groups[1:], jnp.zeros_like(groups[:1])], axis=0)
    return jnp.concatenate([groups, later], axis=1)


def from_owners(slots, share):
    later = jnp.concatenate([jnp.zeros_like(slots[:1, share:]), slots[:-1, share:]], axis=0)
    return (slots[:, :share] + later).reshape(-1, slots.shape[-1])


def on_device_whole(
    tokens,
    seg_ids,
    routed_index,
    gain_attn,
    w_qkv,
    w_out,
    gain_mlp,
    w_up,
    w_down,
    w_router,
    out_grad,
):
    f32, bf16 = jnp.float32, jnp.bfloat16
    seq_count, group_len, model_width = tokens.shape
    routed_len = routed_index.shape[1]
    dev_count = lax.axis_size("seq")
    dev_index = lax.axis_index("seq")
    core = lax.axis_index("tp") % 2
    side = lax.axis_index("tp") // 2
    share = routed_len // dev_count
    half_width = model_width // 2
    quarter_width = half_width // 2

    padded_index = jnp.concatenate(
        [routed_index, jnp.full((seq_count, share), -1, jnp.int32)], axis=1
    )
    slots = lax.dynamic_slice(padded_index, (0, dev_index * share), (seq_count, 2 * share))
    offsets = jnp.arange(group_len, dtype=jnp.int32)
    table = ((slots - dev_index * group_len)[:, :, None] == offsets).astype(bf16)

    index_row = lax.dynamic_index_in_dim(routed_index, dev_index, 0, False)
    seg_row = lax.dynamic_index_in_dim(seg_ids, dev_index, 0, False)
    seg_routed = sum(
        (index_row >= jnp.sum((seg_row < t).astype(jnp.int32))).astype(jnp.int32)
        for t in range(1, 4)
    )
    def pick(source, first, width):
        own = lax.dynamic_slice_in_dim(source, first, width, 2)
        return compact(table, own).astype(bf16)

    def exchange(own):
        return lax.all_to_all(own, "seq", 0, 0, tiled=True)

    def settle(slots):
        own = from_owners(slots, share)
        if own.shape[1] < half_width:
            own = join_halves(own, tp_permute(own, 2), side)
        return join_halves(own, tp_permute(own, 1), core)

    slots, seg_routed, picked_grads = lax.optimization_barrier(
        (
            exchange(pick(tokens, core * half_width, half_width)),
            seg_routed,
            pick(out_grad, core * half_width + side * quarter_width, quarter_width),
        )
    )
    routed_rows = settle(slots)

    ranks = jnp.arange(routed_len, dtype=jnp.int32)
    allowed = jnp.logical_and(
        ranks[None, :] <= ranks[:, None], seg_routed[None, :] == seg_routed[:, None]
    )[None]

    rows = routed_rows.astype(f32)
    gain_first = gain_attn.astype(f32)
    gain_second = gain_mlp.astype(f32)
    router = w_router.astype(f32)
    gating = jax.nn.sigmoid(jnp.sum(rows * router, axis=-1, keepdims=True))
    factor_first = lax.rsqrt(jnp.mean(rows * rows, axis=-1, keepdims=True) + 1e-05)
    attn_input = (rows * factor_first * gain_first).astype(bf16)
    weights = jnp.transpose(w_qkv, (1, 0, 2))
    qkv = jnp.einsum("rd,cdh->crh", attn_input, weights, preferred_element_type=f32).astype(bf16)
    head_count = qkv.shape[2] // HEAD_DIM
    scaling = HEAD_DIM ** (-0.5)

    def heads(values):
        return values.reshape(routed_len, head_count, HEAD_DIM)

    queries, keys, values = heads(qkv[0]), heads(qkv[1]), heads(qkv[2])
    raw = jnp.einsum("qhe,khe->hqk", queries, keys, preferred_element_type=f32)
    logits = jnp.where(allowed, raw * scaling, -1e30)
    powered = jnp.exp(logits - jnp.max(logits, axis=-1, keepdims=True))
    probs = powered / jnp.sum(powered, axis=-1, keepdims=True)
    probs_low = probs.astype(bf16)
    mixed = jnp.einsum("hqk,khe->qhe", probs_low, values, preferred_element_type=f32)
    mixed = mixed.reshape(routed_len, -1).astype(bf16)
    mixed, grad_slots = lax.optimization_barrier((mixed, exchange(picked_grads)))
    attn_half = tp_start(jnp.dot(mixed, w_out, preferred_element_type=f32), core)
    grad_rows = settle(grad_slots).astype(f32)
    attn_half = tp_cross(attn_half)
    attn_out = tp_join(attn_half, core)

    residual = rows + attn_out
    factor_second = lax.rsqrt(jnp.mean(residual * residual, axis=-1, keepdims=True) + 1e-05)
    mlp_input = (residual * factor_second * gain_second).astype(bf16)
    scaled_grad = gating * grad_rows
    grad_mlp = scaled_grad.astype(bf16)
    pre_act = jnp.dot(mlp_input, w_up, preferred_element_type=f32)
    hidden, gelu_pull = jax.vjp(gelu_tanh, pre_act)
    hidden = hidden.astype(bf16)
    grad_hidden = lax.dot_general(
        grad_mlp, w_down, (((1,), (1,)), ((), ())), preferred_element_type=f32
    )
    grad_pre = gelu_pull(grad_hidden)[0].astype(bf16)
    pull_part = lax.dot_general(
        grad_pre, w_up, (((1,), (1,)), ((), ())), preferred_element_type=f32
    )
    pull_half = tp_start(pull_part, core)
    mlp_half = tp_start(
        jnp.dot(after(hidden, pull_half), w_down, preferred_element_type=f32), core
    )

    def outer(left, right):
        product = lax.dot_general(
            left, right, (((0,), (0,)), ((), ())), preferred_element_type=f32
        )
        return product.astype(bf16)

    mlp_pairs = lax.dot_general(
        jnp.stack([mlp_input, grad_mlp]),
        jnp.stack([grad_pre, hidden]),
        (((1,), (1,)), ((0,), (0,))),
        preferred_element_type=f32,
    ).astype(bf16)

    def mlp_ring(total, step, *others):
        return ring_step(mlp_pairs, 1, core, total, step, *others)

    mlp_ring_0 = mlp_ring(None, 0)
    mlp_ring_1 = mlp_ring(mlp_ring_0, 1)
    pull_half, mlp_half = lax.optimization_barrier(
        (tp_cross(pull_half, mlp_half), mlp_half)
    )
    quarter = pick_half(attn_half, side).astype(f32) + pick_half(mlp_half, side).astype(f32)
    branch_part = quarter + tp_permute(pick_half(mlp_half, 1 - side), 2).astype(f32)
    grad_mlp_input = tp_join(pull_half, core, *mlp_ring_1)

    weighted = grad_mlp_input * gain_second
    grad_residual = factor_second * weighted - residual * factor_second**3 * jnp.mean(
        residual * weighted, axis=-1, keepdims=True
    )
    grad_gain_mlp = jnp.sum(grad_mlp_input * residual * factor_second, axis=0)
    grad_attn = (grad_residual + scaled_grad).astype(bf16)
    grad_mixed = lax.dot_general(
        grad_attn, w_out, (((1,), (1,)), ((), ())), preferred_element_type=f32
    ).astype(bf16)
    grad_heads = heads(grad_mixed)
    grad_probs = jnp.einsum("qhe,khe->hqk", grad_heads, values, preferred_element_type=f32)
    inner_sum = jnp.sum(probs * grad_probs, axis=-1, keepdims=True)
    grad_raw = (probs * (grad_probs - inner_sum) * scaling).astype(bf16)
    def flat(products):
        return products.reshape(routed_len, -1).astype(bf16)

    grad_query = flat(jnp.einsum("hqk,khe->qhe", grad_raw, keys, preferred_element_type=f32))
    grad_key = flat(jnp.einsum("hqk,qhe->khe", grad_raw, queries, preferred_element_type=f32))
    grad_value = flat(jnp.einsum("hqk,qhe->khe", probs_low, grad_heads, preferred_element_type=f32))
    mlp_ring_2 = mlp_ring(mlp_ring_1, 2)
    grad_query, grad_key, grad_value, branch_part, mlp_ring_2 = lax.optimization_barrier(
        (grad_query, grad_key, grad_value, branch_part, mlp_ring_2)
    )
    grad_parts = (grad_query, grad_key, grad_value)
    update = (gating * branch_part).astype(bf16)
    score = jnp.sum(pick_half(pick_half(grad_rows, core), side) * branch_part, axis=-1)
    score = score + tp_permute(score, 1)
    score = score + tp_permute(score, 2)
    down_part = sum(
        lax.dot_general(
            grad_parts[c], weights[c], (((1,), (1,)), ((), ())), preferred_element_type=f32
        )
        for c in range(3)
    )
    input_half = tp_start(down_part, core)

    grad_rows_flat = jnp.concatenate(grad_parts, axis=1)
    attn_pairs = jnp.concatenate(
        [outer(attn_input, grad_rows_flat), outer(grad_attn, mixed)], axis=1
    )

    def attn_ring(total, step, *others):
        return ring_step(attn_pairs, 0, core, total, step, *others)

    attn_ring_0 = attn_ring(None, 0)

    input_half, score = lax.optimization_barrier((tp_cross(input_half), score))
    grad_score = gating * (1.0 - gating) * score[:, None]
    grad_attn_input = tp_join(input_half, core)
    weighted = grad_attn_input * gain_first
    grad_norm = factor_first * weighted - rows * factor_first**3 * jnp.mean(
        rows * weighted, axis=-1, keepdims=True
    )
    grad_gain_attn = jnp.sum(grad_attn_input * rows * factor_first, axis=0)
    grad_router = jnp.sum(grad_score * rows, axis=0)
    grad_routed_in = (grad_residual + grad_norm + grad_score * router).astype(bf16)

    small = jnp.stack([grad_gain_attn, grad_gain_mlp, grad_router]).astype(bf16)
    small = small.reshape(3, dev_count, -1).transpose(1, 0, 2)
    small = jnp.pad(small, ((0, 0), (0, 13), (0, half_width - small.shape[2])))
    grads_part = pick_half(pick_half(grad_routed_in, core), side)
    pieces = to_owners(jnp.concatenate([update, grads_part], axis=1), share)
    sent = jnp.concatenate([pieces, small], axis=1)
    got = lax.all_to_all(sent, "seq", 0, 0, tiled=True)
    mlp_total = mlp_ring(mlp_ring_2, 3, sent)
    attn_total = attn_ring(attn_ring_0, 1, sent)
    for step in range(4, dev_count // 2 + 1):
        mlp_total = mlp_ring(mlp_total, step)
    for step in range(2, dev_count // 2 + 1):
        if step == 2:
            attn_total, got = lax.optimization_barrier((attn_total, got))
        attn_total = attn_ring(attn_total, step)
    grad_up, grad_down = mlp_total[0], mlp_total[1].T
    split = 3 * mixed.shape[1]
    grad_qkv = attn_total[:, :split].reshape(-1, 3, mixed.shape[1])
    grad_out = attn_total[:, split:].T

    small = jnp.sum(got[:, 2 * share : 2 * share + 3, : model_width // dev_count].astype(f32), axis=0)
    width = half_width // 2

    def gather(part):
        part = join_halves(part, tp_permute(part, 2), side)
        return join_halves(part, tp_permute(part, 1), core)

    block_rows = gather(got[:, : 2 * share, :width])
    grad_slots = gather(got[:, : 2 * share, width:])
    block_out = (tokens.astype(f32) + spread(table, block_rows)).astype(bf16)
    grad_tokens = out_grad.astype(f32) + spread(table, grad_slots)
    return (
        block_out,
        grad_tokens,
        small[0],
        grad_qkv,
        grad_out,
        small[1],
        grad_up,
        grad_down,
        small[2],
    )


def solution(mesh):
    def on_device(*arrays):
        seq_count, routed_len = arrays[2].shape
        dev_count = mesh.shape["seq"]
        whole = seq_count == dev_count and mesh.shape["tp"] == 4 and dev_count % 2 == 0
        body = on_device_whole if whole else on_device_split
        return body(*arrays)

    return jax.shard_map(
        on_device,
        mesh=mesh,
        in_specs=(
            P(None, "seq", None),
            P(),
            P(),
            P(),
            P(None, None, "tp"),
            P("tp", None),
            P(),
            P(None, "tp"),
            P("tp", None),
            P(),
            P(None, "seq", None),
        ),
        out_specs=(
            P(None, "seq", None),
            P(None, "seq", None),
            P("seq"),
            P("seq", None, "tp"),
            P("tp", "seq"),
            P("seq"),
            P("seq", "tp"),
            P("tp", "seq"),
            P("seq"),
        ),
        check_vma=False,
    )
```

```python
import jax
import jax.numpy as jnp
from jax import lax
from jax.experimental import pallas as pl
from jax.experimental.pallas import tpu as pltpu
from jax.sharding import PartitionSpec as P

HEAD_DIM = 64


precise = lax.Precision.HIGHEST


def normed(values, gain):
    factor = lax.rsqrt(jnp.mean(values * values, axis=-1, keepdims=True) + 1e-05)
    return values * factor * gain


def gelu_tanh(values):
    return jax.nn.gelu(values, approximate=True)


def match_table(positions, usable, anchor, extent):
    offsets = jnp.arange(extent, dtype=jnp.int32)
    hits = (positions - anchor)[:, :, None] == offsets[None, None, :]
    return jnp.logical_and(hits, usable[:, :, None]).astype(jnp.bfloat16)


def compact(table, source):
    return jnp.einsum("sqc,scd->sqd", table, source, preferred_element_type=jnp.float32)


def spread(table, routed_rows):
    return jnp.einsum("sqc,sqd->scd", table, routed_rows, preferred_element_type=jnp.float32)


def on_device_split(
    tokens,
    seg_ids,
    routed_index,
    gain_attn,
    w_qkv,
    w_out,
    gain_mlp,
    w_up,
    w_down,
    w_router,
    out_grad,
):
    seq_count, group_len, model_width = tokens.shape
    routed_len = routed_index.shape[1]
    dev_count = lax.axis_size("seq")
    dev_index = lax.axis_index("seq")
    per_dev = routed_len // dev_count
    group_base = dev_index * group_len
    seg_routed = jnp.take_along_axis(seg_ids, routed_index, axis=1)
    capacity = 2 * per_dev
    slot_ids = jnp.arange(capacity, dtype=jnp.int32)
    first_rank = jnp.sum((routed_index < group_base).astype(jnp.int32), axis=1)
    group_count = (
        jnp.sum((routed_index < group_base + group_len).astype(jnp.int32), axis=1) - first_rank
    )
    query_rank = first_rank[:, None] + slot_ids[None, :]
    query_valid = slot_ids[None, :] < group_count[:, None]
    clipped = jnp.minimum(query_rank, routed_len - 1)
    query_pos = jnp.take_along_axis(routed_index, clipped, axis=1)
    own_table = match_table(query_pos, query_valid, group_base, group_len)
    routed_rows = compact(own_table, tokens).astype(jnp.bfloat16)
    routed_grads = compact(own_table, out_grad).astype(jnp.bfloat16)
    query_seg = jnp.take_along_axis(seg_routed, clipped, axis=1)
    bounds = jnp.arange(dev_count, dtype=jnp.int32) * group_len
    firsts = jnp.sum((routed_index[:, :, None] < bounds[None, None, :]).astype(jnp.int32), axis=1)
    next_firsts = jnp.concatenate(
        [firsts[:, 1:], jnp.full((seq_count, 1), routed_len, jnp.int32)], axis=1
    )
    key_rank = (firsts[:, :, None] + slot_ids[None, None, :]).reshape(seq_count, -1)
    key_valid = (slot_ids[None, None, :] < (next_firsts - firsts)[:, :, None]).reshape(
        seq_count, -1
    )
    key_seg = jnp.take_along_axis(seg_routed, jnp.minimum(key_rank, routed_len - 1), axis=1)
    allowed = jnp.logical_and(
        key_rank[:, None, :] <= query_rank[:, :, None], key_seg[:, None, :] == query_seg[:, :, None]
    )
    allowed = jnp.logical_and(allowed, key_valid[:, None, :])[:, None]
    rows_float = routed_rows.astype(jnp.float32)
    gain_first = gain_attn.astype(jnp.float32)
    gain_second = gain_mlp.astype(jnp.float32)
    router_score = jnp.einsum(
        "sqd,d->sq", routed_rows, w_router, preferred_element_type=jnp.float32
    )
    gating = jax.nn.sigmoid(router_score)
    attn_input = normed(rows_float, gain_first).astype(jnp.bfloat16)
    qkv_rows = jnp.einsum(
        "sqd,dch->sqch", attn_input, w_qkv, preferred_element_type=jnp.float32
    ).astype(jnp.bfloat16)
    query_count = qkv_rows.shape[1]
    head_count = qkv_rows.shape[3] // HEAD_DIM
    query_flat = qkv_rows[:, :, 0]
    queries = query_flat.reshape(seq_count, query_count, head_count, HEAD_DIM)
    key_pair = (qkv_rows[:, :, 1], qkv_rows[:, :, 2])
    all_keys = lax.all_gather(key_pair[0], "seq", axis=1, tiled=True)
    all_values = lax.all_gather(key_pair[1], "seq", axis=1, tiled=True)
    key_count = all_keys.shape[1]
    all_keys = all_keys.reshape(seq_count, key_count, head_count, HEAD_DIM)
    all_values = all_values.reshape(seq_count, key_count, head_count, HEAD_DIM)
    scaling = HEAD_DIM ** (-0.5)

    def masked_logits():
        raw_scores = jnp.einsum(
            "sqhe,skhe->shqk", queries, all_keys, preferred_element_type=jnp.float32
        )
        return jnp.where(allowed, raw_scores * scaling, -1e30)

    logits = masked_logits()
    row_peak = jnp.max(logits, axis=-1, keepdims=True)
    powered = jnp.exp(logits - row_peak)
    row_total = jnp.sum(powered, axis=-1, keepdims=True)
    log_total = row_peak + jnp.log(row_total)
    probs_low = (powered / row_total).astype(jnp.bfloat16)
    mixed = jnp.einsum("shqk,skhe->sqhe", probs_low, all_values, preferred_element_type=jnp.float32)
    mixed = mixed.reshape(seq_count, query_count, -1).astype(jnp.bfloat16)
    attn_out = lax.psum(
        jnp.einsum("sqh,hd->sqd", mixed, w_out, preferred_element_type=jnp.float32).astype(
            jnp.bfloat16
        ),
        "tp",
    ).astype(jnp.float32)
    residual = rows_float + attn_out
    mlp_input = normed(residual, gain_second).astype(jnp.bfloat16)
    pre_act = jnp.einsum("sqd,df->sqf", mlp_input, w_up, preferred_element_type=jnp.float32)
    hidden = gelu_tanh(pre_act).astype(jnp.bfloat16)
    mlp_out = lax.psum(
        jnp.einsum("sqf,fd->sqd", hidden, w_down, preferred_element_type=jnp.float32).astype(
            jnp.bfloat16
        ),
        "tp",
    ).astype(jnp.float32)
    branch = attn_out + mlp_out
    update_rows = (gating[:, :, None] * branch).astype(jnp.bfloat16)
    block_out = (tokens.astype(jnp.float32) + spread(own_table, update_rows)).astype(jnp.bfloat16)
    grad_rows = routed_grads.astype(jnp.float32)
    scaled_grad = gating[:, :, None] * grad_rows
    grad_score = jnp.sum(grad_rows * branch, axis=-1) * gating * (1.0 - gating)
    grad_mlp = scaled_grad.astype(jnp.bfloat16)
    grad_down = jnp.einsum("sqf,sqd->fd", hidden, grad_mlp, preferred_element_type=jnp.float32)
    grad_hidden = jnp.einsum("sqd,fd->sqf", grad_mlp, w_down, preferred_element_type=jnp.float32)
    gelu_pull = jax.vjp(gelu_tanh, pre_act)[1]
    grad_pre = gelu_pull(grad_hidden)[0].astype(jnp.bfloat16)
    grad_up = jnp.einsum("sqd,sqf->df", mlp_input, grad_pre, preferred_element_type=jnp.float32)
    grad_mlp_input = lax.psum(
        jnp.einsum("sqf,df->sqd", grad_pre, w_up, preferred_element_type=jnp.float32).astype(
            jnp.bfloat16
        ),
        "tp",
    ).astype(jnp.float32)
    second_pull = jax.vjp(normed, residual, gain_second)[1]
    grad_residual, grad_gain_mlp = second_pull(grad_mlp_input)
    grad_attn = (grad_residual + scaled_grad).astype(jnp.bfloat16)
    grad_out = jnp.einsum("sqh,sqd->hd", mixed, grad_attn, preferred_element_type=jnp.float32)
    grad_mixed_flat = jnp.einsum(
        "sqd,hd->sqh", grad_attn, w_out, preferred_element_type=jnp.float32
    ).astype(jnp.bfloat16)
    grad_mixed = grad_mixed_flat.reshape(seq_count, query_count, head_count, HEAD_DIM)
    probs_again = jnp.where(allowed, jnp.exp(masked_logits() - log_total), 0.0)
    grad_probs = jnp.einsum(
        "sqhe,skhe->shqk", grad_mixed, all_values, preferred_element_type=jnp.float32
    )
    inner_sum = jnp.sum(probs_again * grad_probs, axis=-1, keepdims=True)
    grad_raw = (probs_again * (grad_probs - inner_sum) * scaling).astype(jnp.bfloat16)
    grad_query = jnp.einsum(
        "shqk,skhe->sqhe", grad_raw, all_keys, preferred_element_type=jnp.float32
    )
    grad_query = grad_query.reshape(seq_count, query_count, -1).astype(jnp.bfloat16)
    probs_again_low = probs_again.astype(jnp.bfloat16)
    key_part = jnp.einsum(
        "shqk,sqhe->skhe", grad_raw, queries, preferred_element_type=jnp.float32
    ).reshape(seq_count, key_count, -1)
    value_part = jnp.einsum(
        "shqk,sqhe->skhe", probs_again_low, grad_mixed, preferred_element_type=jnp.float32
    ).reshape(seq_count, key_count, -1)
    key_pair = (key_part, value_part)
    grad_keys = lax.psum_scatter(key_pair[0], "seq", scatter_dimension=1, tiled=True)
    grad_values = lax.psum_scatter(key_pair[1], "seq", scatter_dimension=1, tiled=True)
    grad_qkv_rows = jnp.stack(
        [grad_query, grad_keys.astype(jnp.bfloat16), grad_values.astype(jnp.bfloat16)], axis=2
    )
    grad_qkv = jnp.einsum(
        "sqd,sqch->dch", attn_input, grad_qkv_rows, preferred_element_type=jnp.float32
    )
    grad_attn_input = lax.psum(
        jnp.einsum(
            "sqch,dch->sqd", grad_qkv_rows, w_qkv, preferred_element_type=jnp.float32
        ).astype(jnp.bfloat16),
        "tp",
    ).astype(jnp.float32)
    first_pull = jax.vjp(normed, rows_float, gain_first)[1]
    grad_norm, grad_gain_attn = first_pull(grad_attn_input)
    grad_router = jnp.einsum("sq,sqd->d", grad_score, rows_float, precision=precise)
    grad_routed_in = (
        grad_residual + grad_norm + grad_score[:, :, None] * w_router.astype(jnp.float32)
    ).astype(jnp.bfloat16)
    grad_tokens = out_grad.astype(jnp.float32) + spread(own_table, grad_routed_in)
    reduced = (
        lax.psum_scatter(grad_gain_attn, "seq", scatter_dimension=0, tiled=True),
        lax.psum_scatter(grad_qkv, "seq", scatter_dimension=0, tiled=True),
        lax.psum_scatter(grad_out, "seq", scatter_dimension=1, tiled=True),
        lax.psum_scatter(grad_gain_mlp, "seq", scatter_dimension=0, tiled=True),
        lax.psum_scatter(grad_up, "seq", scatter_dimension=0, tiled=True),
        lax.psum_scatter(grad_down, "seq", scatter_dimension=1, tiled=True),
        lax.psum_scatter(grad_router, "seq", scatter_dimension=0, tiled=True),
    )
    return (block_out, grad_tokens) + tuple(reduced)


def ring_order(size):
    return list(range(0, size, 2)) + list(range(size - 1, 0, -2))


def ring_place(index, size):
    return jnp.where(index % 2 == 0, index // 2, size - 1 - index // 2)


def ring_owner(place, size):
    place = place % size
    return jnp.where(place < size // 2, 2 * place, 2 * (size - place) - 1)


def ring_permute(values, sign):
    order = ring_order(lax.axis_size("seq"))
    size, width = len(order), lax.axis_size("tp")
    pairs = []
    for i in range(size):
        for t in range(width):
            there = (i + sign * (1 - 2 * (t % 2))) % size
            pairs.append((order[i] * width + t, order[there] * width + t))
    return lax.ppermute(values, ("seq", "tp"), pairs)


def after(value, *others):
    return lax.optimization_barrier((value,) + others)[0]


def ring_chunk(whole, axis, core, distance):
    size = lax.axis_size("seq")
    place = ring_place(lax.axis_index("seq"), size)
    width = whole.shape[axis] // size
    owner = ring_owner(place + size + distance * (1 - 2 * core), size)
    return lax.dynamic_slice_in_dim(whole, owner * width, width, axis)


def ring_send(state, step):
    near = lax.axis_size("seq") // 2 - 1
    ahead = ring_permute(state[0], 1)
    return ahead, ring_permute(state[1], -1) if step <= near else state[1]


def ring_add(whole, axis, core, moved, step):
    size = lax.axis_size("seq")
    far, near = size // 2, size // 2 - 1
    f32, bf16 = jnp.float32, jnp.bfloat16

    def chunk(distance):
        return ring_chunk(whole, axis, core, distance)

    if step == 0:
        return chunk(far), chunk(-near)
    ahead, behind = moved
    if step == far:
        return chunk(0).astype(f32) + ahead.astype(f32) + behind.astype(f32)
    ahead = (ahead.astype(f32) + chunk(far - step).astype(f32)).astype(bf16)
    if step < near:
        behind = (behind.astype(f32) + chunk(step - near).astype(f32)).astype(bf16)
    return ahead, behind


def ring_step(whole, axis, core, state, step, *others):
    moved = None if step == 0 else ring_send(state, step)
    if others:
        moved = lax.optimization_barrier(moved + others)[:2]
    return ring_add(whole, axis, core, moved, step)


def tp_permute(values, mask):
    size = lax.axis_size("tp")
    return lax.ppermute(values, "tp", [(i, i ^ mask) for i in range(size)])


def pick_half(values, which):
    width = values.shape[-1] // 2
    return jnp.where(which == 0, values[..., :width], values[..., width:])


def join_halves(own, other, which):
    return jnp.where(
        which == 0,
        jnp.concatenate([own, other], axis=-1),
        jnp.concatenate([other, own], axis=-1),
    )


def tp_start(partial, which):
    narrow = partial.astype(jnp.bfloat16)
    moved = tp_permute(pick_half(narrow, 1 - which), 1)
    half = pick_half(partial, which) + moved.astype(jnp.float32)
    return half.astype(jnp.bfloat16)


def tp_cross(half, *others):
    moved = after(tp_permute(half, 2), *others)
    return (half.astype(jnp.float32) + moved.astype(jnp.float32)).astype(jnp.bfloat16)


def tp_join(half, which, *others):
    return join_halves(half, after(tp_permute(half, 1), *others), which).astype(jnp.float32)


def to_owners(rows, share):
    groups = rows.reshape(-1, share, rows.shape[-1])
    later = jnp.concatenate([groups[1:], jnp.zeros_like(groups[:1])], axis=0)
    return jnp.concatenate([groups, later], axis=1)


def from_owners(slots, share):
    later = jnp.concatenate([jnp.zeros_like(slots[:1, share:]), slots[:-1, share:]], axis=0)
    return (slots[:, :share] + later).reshape(-1, slots.shape[-1])


def times(left, right, left_axis, right_axis):
    return lax.dot_general(
        left,
        right,
        (((left_axis,), (right_axis,)), ((), ())),
        preferred_element_type=jnp.float32,
    )


def head_lanes(lanes, part):
    return lax.broadcasted_iota(jnp.int32, (1, lanes), 1) // HEAD_DIM == part


def forward_kernel(qkv_ref, allowed_ref, probs_ref, mixed_ref):
    width = mixed_ref.shape[1]
    lanes, each = 2 * HEAD_DIM, 2
    allowed = allowed_ref[...] != 0
    for block in range(width // lanes):
        queries, keys, values = (
            qkv_ref[:, c * width + block * lanes : c * width + (block + 1) * lanes]
            for c in range(3)
        )
        mixed = None
        for part in range(each):
            mine = head_lanes(lanes, part)
            raw = times(jnp.where(mine, queries, jnp.zeros_like(queries)), keys, 1, 1)
            logits = jnp.where(allowed, raw * HEAD_DIM ** (-0.5), -1e30)
            powered = jnp.exp(logits - jnp.max(logits, axis=-1, keepdims=True))
            probs = powered / jnp.sum(powered, axis=-1, keepdims=True)
            probs_ref[block * each + part] = probs
            product = times(probs.astype(jnp.bfloat16), values, 1, 0)
            mixed = product if part == 0 else jnp.where(mine, product, mixed)
        mixed_ref[:, block * lanes : (block + 1) * lanes] = mixed.astype(jnp.bfloat16)


def backward_kernel(qkv_ref, probs_ref, grad_ref, out_ref):
    width = grad_ref.shape[1]
    lanes, each = 2 * HEAD_DIM, 2
    for block in range(width // lanes):
        queries, keys, values = (
            qkv_ref[:, c * width + block * lanes : c * width + (block + 1) * lanes]
            for c in range(3)
        )
        grads = grad_ref[:, block * lanes : (block + 1) * lanes]
        totals = None
        for part in range(each):
            mine = head_lanes(lanes, part)
            probs = probs_ref[block * each + part]
            grad_probs = times(jnp.where(mine, grads, jnp.zeros_like(grads)), values, 1, 1)
            inner_sum = jnp.sum(probs * grad_probs, axis=-1, keepdims=True)
            grad_raw = probs * (grad_probs - inner_sum) * HEAD_DIM ** (-0.5)
            grad_raw = grad_raw.astype(jnp.bfloat16)
            products = (
                times(grad_raw, keys, 1, 0),
                times(grad_raw, queries, 0, 0),
                times(probs.astype(jnp.bfloat16), grads, 0, 0),
            )
            if part == 0:
                totals = products
            else:
                totals = tuple(jnp.where(mine, new, old) for new, old in zip(products, totals))
        for c in range(3):
            first = c * width + block * lanes
            out_ref[:, first : first + lanes] = totals[c].astype(jnp.bfloat16)


def kernel_cost(rows, width, count):
    return pl.CostEstimate(
        flops=2 * count * rows * rows * width,
        bytes_accessed=4 * rows * rows * width // HEAD_DIM + 8 * rows * width,
        transcendentals=rows * rows * width // HEAD_DIM,
    )


def attend(qkv, allowed):
    rows, width = qkv.shape[0], qkv.shape[1] // 3
    return pl.pallas_call(
        forward_kernel,
        out_shape=(
            jax.ShapeDtypeStruct((width // HEAD_DIM, rows, rows), jnp.float32),
            jax.ShapeDtypeStruct((rows, width), jnp.bfloat16),
        ),
        cost_estimate=kernel_cost(rows, width, 2),
    )(qkv, allowed)


def attend_back(qkv, probs, grads):
    rows, width = grads.shape
    return pl.pallas_call(
        backward_kernel,
        out_shape=jax.ShapeDtypeStruct(qkv.shape, jnp.bfloat16),
        cost_estimate=kernel_cost(rows, width, 5),
    )(qkv, probs, grads)


def on_device_whole(
    tokens,
    seg_ids,
    routed_index,
    gain_attn,
    w_qkv,
    w_out,
    gain_mlp,
    w_up,
    w_down,
    w_router,
    out_grad,
):
    f32, bf16 = jnp.float32, jnp.bfloat16
    seq_count, group_len, model_width = tokens.shape
    routed_len = routed_index.shape[1]
    dev_count = lax.axis_size("seq")
    dev_index = lax.axis_index("seq")
    core = lax.axis_index("tp") % 2
    side = lax.axis_index("tp") // 2
    share = routed_len // dev_count
    half_width = model_width // 2
    quarter_width = half_width // 2

    padded_index = jnp.concatenate(
        [routed_index, jnp.full((seq_count, share), -1, jnp.int32)], axis=1
    )
    slots = lax.dynamic_slice(padded_index, (0, dev_index * share), (seq_count, 2 * share))
    offsets = jnp.arange(group_len, dtype=jnp.int32)
    table = ((slots - dev_index * group_len)[:, :, None] == offsets).astype(bf16)

    index_row = lax.dynamic_index_in_dim(routed_index, dev_index, 0, False)
    seg_row = lax.dynamic_index_in_dim(seg_ids, dev_index, 0, False)
    seg_routed = sum(
        (index_row >= jnp.sum((seg_row < t).astype(jnp.int32))).astype(jnp.int32)
        for t in range(1, 4)
    )
    def pick(source, first, width):
        own = lax.dynamic_slice_in_dim(source, first, width, 2)
        return compact(table, own).astype(bf16)

    def exchange(own):
        return lax.all_to_all(own, "seq", 0, 0, tiled=True)

    def settle(slots):
        own = from_owners(slots, share)
        if own.shape[1] < half_width:
            own = join_halves(own, tp_permute(own, 2), side)
        return join_halves(own, tp_permute(own, 1), core)

    slots, seg_routed, picked_grads, weights = lax.optimization_barrier(
        (
            exchange(pick(tokens, core * half_width, half_width)),
            seg_routed,
            pick(out_grad, core * half_width + side * quarter_width, quarter_width),
            w_qkv.reshape(model_width, -1),
        )
    )
    routed_rows = settle(slots)

    ranks = jnp.arange(routed_len, dtype=jnp.int32)
    allowed = jnp.logical_and(
        ranks[None, :] <= ranks[:, None], seg_routed[None, :] == seg_routed[:, None]
    )

    rows = routed_rows.astype(f32)
    gain_first = gain_attn.astype(f32)
    gain_second = gain_mlp.astype(f32)
    router = w_router.astype(f32)
    gating = jax.nn.sigmoid(jnp.sum(rows * router, axis=-1, keepdims=True))
    factor_first = lax.rsqrt(jnp.mean(rows * rows, axis=-1, keepdims=True) + 1e-05)
    attn_input = (rows * factor_first * gain_first).astype(bf16)
    qkv = jnp.dot(attn_input, weights, preferred_element_type=f32).astype(bf16)
    probs, mixed = attend(qkv, allowed.astype(jnp.int32))
    mixed, grad_slots = lax.optimization_barrier((mixed, exchange(picked_grads)))
    attn_half = tp_start(jnp.dot(mixed, w_out, preferred_element_type=f32), core)
    grad_rows = settle(grad_slots).astype(f32)
    attn_half = tp_cross(attn_half)
    attn_out = tp_join(attn_half, core)

    residual = rows + attn_out
    factor_second = lax.rsqrt(jnp.mean(residual * residual, axis=-1, keepdims=True) + 1e-05)
    mlp_input = (residual * factor_second * gain_second).astype(bf16)
    scaled_grad = gating * grad_rows
    grad_mlp = scaled_grad.astype(bf16)
    pre_act = jnp.dot(mlp_input, w_up, preferred_element_type=f32)
    hidden, gelu_pull = jax.vjp(gelu_tanh, pre_act)
    hidden = hidden.astype(bf16)
    grad_hidden = lax.dot_general(
        grad_mlp, w_down, (((1,), (1,)), ((), ())), preferred_element_type=f32
    )
    grad_pre = gelu_pull(grad_hidden)[0].astype(bf16)
    pull_part = lax.dot_general(
        grad_pre, w_up, (((1,), (1,)), ((), ())), preferred_element_type=f32
    )
    pull_half = tp_start(pull_part, core)
    mlp_half = tp_start(
        jnp.dot(after(hidden, pull_half), w_down, preferred_element_type=f32), core
    )

    def outer(left, right):
        product = lax.dot_general(
            left, right, (((0,), (0,)), ((), ())), preferred_element_type=f32
        )
        return product.astype(bf16)

    mlp_pairs = lax.dot_general(
        jnp.stack([mlp_input, grad_mlp]),
        jnp.stack([grad_pre, hidden]),
        (((1,), (1,)), ((0,), (0,))),
        preferred_element_type=f32,
    ).astype(bf16)

    def mlp_ring(total, step, *others):
        return ring_step(mlp_pairs, 1, core, total, step, *others)

    mlp_ring_0 = mlp_ring(None, 0)
    mlp_ring_1 = mlp_ring(mlp_ring_0, 1)
    pull_half, mlp_half = lax.optimization_barrier(
        (tp_cross(pull_half, mlp_half), mlp_half)
    )
    quarter = pick_half(attn_half, side).astype(f32) + pick_half(mlp_half, side).astype(f32)
    branch_part = quarter + tp_permute(pick_half(mlp_half, 1 - side), 2).astype(f32)
    grad_mlp_input = tp_join(pull_half, core, *mlp_ring_1)

    weighted = grad_mlp_input * gain_second
    grad_residual = factor_second * weighted - residual * factor_second**3 * jnp.mean(
        residual * weighted, axis=-1, keepdims=True
    )
    grad_gain_mlp = jnp.sum(grad_mlp_input * residual * factor_second, axis=0)
    grad_attn = (grad_residual + scaled_grad).astype(bf16)
    grad_mixed = lax.dot_general(
        grad_attn, w_out, (((1,), (1,)), ((), ())), preferred_element_type=f32
    ).astype(bf16)
    grad_parts = attend_back(qkv, probs, grad_mixed)
    mlp_ring_2 = mlp_ring(mlp_ring_1, 2)
    grad_parts, branch_part = lax.optimization_barrier((grad_parts, branch_part))
    update = (gating * branch_part).astype(bf16)
    score = jnp.sum(pick_half(pick_half(grad_rows, core), side) * branch_part, axis=-1)
    score = score + tp_permute(score, 1)
    score = score + tp_permute(score, 2)
    down_part = lax.dot_general(
        grad_parts, weights, (((1,), (1,)), ((), ())), preferred_element_type=f32
    )
    input_half = tp_start(down_part, core)

    attn_pairs = jnp.concatenate(
        [outer(attn_input, grad_parts), outer(grad_attn, mixed)], axis=1
    )

    def attn_ring(total, step, *others):
        return ring_step(attn_pairs, 0, core, total, step, *others)

    attn_ring_0 = attn_ring(None, 0)
    attn_sent = ring_send(attn_ring_0, 1)

    input_half, score = lax.optimization_barrier((tp_cross(input_half, *mlp_ring_2, *attn_ring_0), score))
    grad_score = gating * (1.0 - gating) * score[:, None]
    grad_attn_input = tp_join(input_half, core)
    weighted = grad_attn_input * gain_first
    grad_norm = factor_first * weighted - rows * factor_first**3 * jnp.mean(
        rows * weighted, axis=-1, keepdims=True
    )
    grad_gain_attn = jnp.sum(grad_attn_input * rows * factor_first, axis=0)
    grad_router = jnp.sum(grad_score * rows, axis=0)
    grad_routed_in = (grad_residual + grad_norm + grad_score * router).astype(bf16)

    small = jnp.stack([grad_gain_attn, grad_gain_mlp, grad_router]).astype(bf16)
    small = small.reshape(3, dev_count, -1).transpose(1, 0, 2)
    small = jnp.pad(small, ((0, 0), (0, 13), (0, half_width - small.shape[2])))
    grads_part = pick_half(pick_half(grad_routed_in, core), side)
    pieces = to_owners(jnp.concatenate([update, grads_part], axis=1), share)
    sent = jnp.concatenate([pieces, small], axis=1)
    sent, *attn_sent = lax.optimization_barrier((sent,) + attn_sent)
    got = lax.all_to_all(sent, "seq", 0, 0, tiled=True)
    mlp_total = mlp_ring(mlp_ring_2, 3, sent)
    attn_total = ring_add(attn_pairs, 0, core, attn_sent, 1)
    for step in range(4, dev_count // 2 + 1):
        mlp_total = mlp_ring(mlp_total, step)
    for step in range(2, dev_count // 2 + 1):
        if step == 2:
            attn_total, got = lax.optimization_barrier((attn_total, got))
        attn_total = attn_ring(attn_total, step)
    grad_up, grad_down = mlp_total[0], mlp_total[1].T
    split = 3 * mixed.shape[1]
    grad_qkv = attn_total[:, :split].reshape(-1, 3, mixed.shape[1])
    grad_out = attn_total[:, split:].T

    small = jnp.sum(got[:, 2 * share : 2 * share + 3, : model_width // dev_count].astype(f32), axis=0)
    width = half_width // 2

    def gather(part):
        part = join_halves(part, tp_permute(part, 2), side)
        return join_halves(part, tp_permute(part, 1), core)

    block_rows = gather(got[:, : 2 * share, :width])
    grad_slots = gather(got[:, : 2 * share, width:])
    block_out = (tokens.astype(f32) + spread(table, block_rows)).astype(bf16)
    grad_tokens = out_grad.astype(f32) + spread(table, grad_slots)
    return (
        block_out,
        grad_tokens,
        small[0],
        grad_qkv,
        grad_out,
        small[1],
        grad_up,
        grad_down,
        small[2],
    )


def solution(mesh):
    def on_device(*arrays):
        seq_count, routed_len = arrays[2].shape
        dev_count = mesh.shape["seq"]
        whole = seq_count == dev_count and mesh.shape["tp"] == 4 and dev_count % 2 == 0
        body = on_device_whole if whole else on_device_split
        return body(*arrays)

    return jax.shard_map(
        on_device,
        mesh=mesh,
        in_specs=(
            P(None, "seq", None),
            P(),
            P(),
            P(),
            P(None, None, "tp"),
            P("tp", None),
            P(),
            P(None, "tp"),
            P("tp", None),
            P(),
            P(None, "seq", None),
        ),
        out_specs=(
            P(None, "seq", None),
            P(None, "seq", None),
            P("seq"),
            P("seq", None, "tp"),
            P("tp", "seq"),
            P("seq"),
            P("seq", "tp"),
            P("tp", "seq"),
            P("seq"),
        ),
        check_vma=False,
    )
```

```python
import jax
import jax.numpy as jnp
from jax import lax
from jax.experimental import pallas as pl
from jax.experimental.pallas import tpu as pltpu
from jax.sharding import PartitionSpec as P

HEAD_DIM = 64


precise = lax.Precision.HIGHEST


def normed(values, gain):
    factor = lax.rsqrt(jnp.mean(values * values, axis=-1, keepdims=True) + 1e-05)
    return values * factor * gain


def gelu_tanh(values):
    return jax.nn.gelu(values, approximate=True)


def match_table(positions, usable, anchor, extent):
    offsets = jnp.arange(extent, dtype=jnp.int32)
    hits = (positions - anchor)[:, :, None] == offsets[None, None, :]
    return jnp.logical_and(hits, usable[:, :, None]).astype(jnp.bfloat16)


def compact(table, source):
    return jnp.einsum("sqc,scd->sqd", table, source, preferred_element_type=jnp.float32)


def spread(table, routed_rows):
    return jnp.einsum("sqc,sqd->scd", table, routed_rows, preferred_element_type=jnp.float32)


def on_device_split(
    tokens,
    seg_ids,
    routed_index,
    gain_attn,
    w_qkv,
    w_out,
    gain_mlp,
    w_up,
    w_down,
    w_router,
    out_grad,
):
    seq_count, group_len, model_width = tokens.shape
    routed_len = routed_index.shape[1]
    dev_count = lax.axis_size("seq")
    dev_index = lax.axis_index("seq")
    per_dev = routed_len // dev_count
    group_base = dev_index * group_len
    seg_routed = jnp.take_along_axis(seg_ids, routed_index, axis=1)
    capacity = 2 * per_dev
    slot_ids = jnp.arange(capacity, dtype=jnp.int32)
    first_rank = jnp.sum((routed_index < group_base).astype(jnp.int32), axis=1)
    group_count = (
        jnp.sum((routed_index < group_base + group_len).astype(jnp.int32), axis=1) - first_rank
    )
    query_rank = first_rank[:, None] + slot_ids[None, :]
    query_valid = slot_ids[None, :] < group_count[:, None]
    clipped = jnp.minimum(query_rank, routed_len - 1)
    query_pos = jnp.take_along_axis(routed_index, clipped, axis=1)
    own_table = match_table(query_pos, query_valid, group_base, group_len)
    routed_rows = compact(own_table, tokens).astype(jnp.bfloat16)
    routed_grads = compact(own_table, out_grad).astype(jnp.bfloat16)
    query_seg = jnp.take_along_axis(seg_routed, clipped, axis=1)
    bounds = jnp.arange(dev_count, dtype=jnp.int32) * group_len
    firsts = jnp.sum((routed_index[:, :, None] < bounds[None, None, :]).astype(jnp.int32), axis=1)
    next_firsts = jnp.concatenate(
        [firsts[:, 1:], jnp.full((seq_count, 1), routed_len, jnp.int32)], axis=1
    )
    key_rank = (firsts[:, :, None] + slot_ids[None, None, :]).reshape(seq_count, -1)
    key_valid = (slot_ids[None, None, :] < (next_firsts - firsts)[:, :, None]).reshape(
        seq_count, -1
    )
    key_seg = jnp.take_along_axis(seg_routed, jnp.minimum(key_rank, routed_len - 1), axis=1)
    allowed = jnp.logical_and(
        key_rank[:, None, :] <= query_rank[:, :, None], key_seg[:, None, :] == query_seg[:, :, None]
    )
    allowed = jnp.logical_and(allowed, key_valid[:, None, :])[:, None]
    rows_float = routed_rows.astype(jnp.float32)
    gain_first = gain_attn.astype(jnp.float32)
    gain_second = gain_mlp.astype(jnp.float32)
    router_score = jnp.einsum(
        "sqd,d->sq", routed_rows, w_router, preferred_element_type=jnp.float32
    )
    gating = jax.nn.sigmoid(router_score)
    attn_input = normed(rows_float, gain_first).astype(jnp.bfloat16)
    qkv_rows = jnp.einsum(
        "sqd,dch->sqch", attn_input, w_qkv, preferred_element_type=jnp.float32
    ).astype(jnp.bfloat16)
    query_count = qkv_rows.shape[1]
    head_count = qkv_rows.shape[3] // HEAD_DIM
    query_flat = qkv_rows[:, :, 0]
    queries = query_flat.reshape(seq_count, query_count, head_count, HEAD_DIM)
    key_pair = (qkv_rows[:, :, 1], qkv_rows[:, :, 2])
    all_keys = lax.all_gather(key_pair[0], "seq", axis=1, tiled=True)
    all_values = lax.all_gather(key_pair[1], "seq", axis=1, tiled=True)
    key_count = all_keys.shape[1]
    all_keys = all_keys.reshape(seq_count, key_count, head_count, HEAD_DIM)
    all_values = all_values.reshape(seq_count, key_count, head_count, HEAD_DIM)
    scaling = HEAD_DIM ** (-0.5)

    def masked_logits():
        raw_scores = jnp.einsum(
            "sqhe,skhe->shqk", queries, all_keys, preferred_element_type=jnp.float32
        )
        return jnp.where(allowed, raw_scores * scaling, -1e30)

    logits = masked_logits()
    row_peak = jnp.max(logits, axis=-1, keepdims=True)
    powered = jnp.exp(logits - row_peak)
    row_total = jnp.sum(powered, axis=-1, keepdims=True)
    log_total = row_peak + jnp.log(row_total)
    probs_low = (powered / row_total).astype(jnp.bfloat16)
    mixed = jnp.einsum("shqk,skhe->sqhe", probs_low, all_values, preferred_element_type=jnp.float32)
    mixed = mixed.reshape(seq_count, query_count, -1).astype(jnp.bfloat16)
    attn_out = lax.psum(
        jnp.einsum("sqh,hd->sqd", mixed, w_out, preferred_element_type=jnp.float32).astype(
            jnp.bfloat16
        ),
        "tp",
    ).astype(jnp.float32)
    residual = rows_float + attn_out
    mlp_input = normed(residual, gain_second).astype(jnp.bfloat16)
    pre_act = jnp.einsum("sqd,df->sqf", mlp_input, w_up, preferred_element_type=jnp.float32)
    hidden = gelu_tanh(pre_act).astype(jnp.bfloat16)
    mlp_out = lax.psum(
        jnp.einsum("sqf,fd->sqd", hidden, w_down, preferred_element_type=jnp.float32).astype(
            jnp.bfloat16
        ),
        "tp",
    ).astype(jnp.float32)
    branch = attn_out + mlp_out
    update_rows = (gating[:, :, None] * branch).astype(jnp.bfloat16)
    block_out = (tokens.astype(jnp.float32) + spread(own_table, update_rows)).astype(jnp.bfloat16)
    grad_rows = routed_grads.astype(jnp.float32)
    scaled_grad = gating[:, :, None] * grad_rows
    grad_score = jnp.sum(grad_rows * branch, axis=-1) * gating * (1.0 - gating)
    grad_mlp = scaled_grad.astype(jnp.bfloat16)
    grad_down = jnp.einsum("sqf,sqd->fd", hidden, grad_mlp, preferred_element_type=jnp.float32)
    grad_hidden = jnp.einsum("sqd,fd->sqf", grad_mlp, w_down, preferred_element_type=jnp.float32)
    gelu_pull = jax.vjp(gelu_tanh, pre_act)[1]
    grad_pre = gelu_pull(grad_hidden)[0].astype(jnp.bfloat16)
    grad_up = jnp.einsum("sqd,sqf->df", mlp_input, grad_pre, preferred_element_type=jnp.float32)
    grad_mlp_input = lax.psum(
        jnp.einsum("sqf,df->sqd", grad_pre, w_up, preferred_element_type=jnp.float32).astype(
            jnp.bfloat16
        ),
        "tp",
    ).astype(jnp.float32)
    second_pull = jax.vjp(normed, residual, gain_second)[1]
    grad_residual, grad_gain_mlp = second_pull(grad_mlp_input)
    grad_attn = (grad_residual + scaled_grad).astype(jnp.bfloat16)
    grad_out = jnp.einsum("sqh,sqd->hd", mixed, grad_attn, preferred_element_type=jnp.float32)
    grad_mixed_flat = jnp.einsum(
        "sqd,hd->sqh", grad_attn, w_out, preferred_element_type=jnp.float32
    ).astype(jnp.bfloat16)
    grad_mixed = grad_mixed_flat.reshape(seq_count, query_count, head_count, HEAD_DIM)
    probs_again = jnp.where(allowed, jnp.exp(masked_logits() - log_total), 0.0)
    grad_probs = jnp.einsum(
        "sqhe,skhe->shqk", grad_mixed, all_values, preferred_element_type=jnp.float32
    )
    inner_sum = jnp.sum(probs_again * grad_probs, axis=-1, keepdims=True)
    grad_raw = (probs_again * (grad_probs - inner_sum) * scaling).astype(jnp.bfloat16)
    grad_query = jnp.einsum(
        "shqk,skhe->sqhe", grad_raw, all_keys, preferred_element_type=jnp.float32
    )
    grad_query = grad_query.reshape(seq_count, query_count, -1).astype(jnp.bfloat16)
    probs_again_low = probs_again.astype(jnp.bfloat16)
    key_part = jnp.einsum(
        "shqk,sqhe->skhe", grad_raw, queries, preferred_element_type=jnp.float32
    ).reshape(seq_count, key_count, -1)
    value_part = jnp.einsum(
        "shqk,sqhe->skhe", probs_again_low, grad_mixed, preferred_element_type=jnp.float32
    ).reshape(seq_count, key_count, -1)
    key_pair = (key_part, value_part)
    grad_keys = lax.psum_scatter(key_pair[0], "seq", scatter_dimension=1, tiled=True)
    grad_values = lax.psum_scatter(key_pair[1], "seq", scatter_dimension=1, tiled=True)
    grad_qkv_rows = jnp.stack(
        [grad_query, grad_keys.astype(jnp.bfloat16), grad_values.astype(jnp.bfloat16)], axis=2
    )
    grad_qkv = jnp.einsum(
        "sqd,sqch->dch", attn_input, grad_qkv_rows, preferred_element_type=jnp.float32
    )
    grad_attn_input = lax.psum(
        jnp.einsum(
            "sqch,dch->sqd", grad_qkv_rows, w_qkv, preferred_element_type=jnp.float32
        ).astype(jnp.bfloat16),
        "tp",
    ).astype(jnp.float32)
    first_pull = jax.vjp(normed, rows_float, gain_first)[1]
    grad_norm, grad_gain_attn = first_pull(grad_attn_input)
    grad_router = jnp.einsum("sq,sqd->d", grad_score, rows_float, precision=precise)
    grad_routed_in = (
        grad_residual + grad_norm + grad_score[:, :, None] * w_router.astype(jnp.float32)
    ).astype(jnp.bfloat16)
    grad_tokens = out_grad.astype(jnp.float32) + spread(own_table, grad_routed_in)
    reduced = (
        lax.psum_scatter(grad_gain_attn, "seq", scatter_dimension=0, tiled=True),
        lax.psum_scatter(grad_qkv, "seq", scatter_dimension=0, tiled=True),
        lax.psum_scatter(grad_out, "seq", scatter_dimension=1, tiled=True),
        lax.psum_scatter(grad_gain_mlp, "seq", scatter_dimension=0, tiled=True),
        lax.psum_scatter(grad_up, "seq", scatter_dimension=0, tiled=True),
        lax.psum_scatter(grad_down, "seq", scatter_dimension=1, tiled=True),
        lax.psum_scatter(grad_router, "seq", scatter_dimension=0, tiled=True),
    )
    return (block_out, grad_tokens) + tuple(reduced)


def ring_order(size):
    return list(range(0, size, 2)) + list(range(size - 1, 0, -2))


def ring_place(index, size):
    return jnp.where(index % 2 == 0, index // 2, size - 1 - index // 2)


def ring_owner(place, size):
    place = place % size
    return jnp.where(place < size // 2, 2 * place, 2 * (size - place) - 1)


def ring_permute(values, sign):
    order = ring_order(lax.axis_size("seq"))
    size, width = len(order), lax.axis_size("tp")
    pairs = []
    for i in range(size):
        for t in range(width):
            there = (i + sign * (1 - 2 * (t % 2))) % size
            pairs.append((order[i] * width + t, order[there] * width + t))
    return lax.ppermute(values, ("seq", "tp"), pairs)


def after(value, *others):
    return lax.optimization_barrier((value,) + others)[0]


def ring_chunk(whole, axis, core, distance):
    size = lax.axis_size("seq")
    place = ring_place(lax.axis_index("seq"), size)
    width = whole.shape[axis] // size
    owner = ring_owner(place + size + distance * (1 - 2 * core), size)
    return lax.dynamic_slice_in_dim(whole, owner * width, width, axis)


def ring_send(state, step):
    near = lax.axis_size("seq") // 2 - 1
    ahead = ring_permute(state[0], 1)
    return ahead, ring_permute(state[1], -1) if step <= near else state[1]


def ring_add(whole, axis, core, moved, step):
    size = lax.axis_size("seq")
    far, near = size // 2, size // 2 - 1
    f32, bf16 = jnp.float32, jnp.bfloat16

    def chunk(distance):
        return ring_chunk(whole, axis, core, distance)

    if step == 0:
        return chunk(far), chunk(-near)
    ahead, behind = moved
    if step == far:
        return chunk(0).astype(f32) + ahead.astype(f32) + behind.astype(f32)
    ahead = (ahead.astype(f32) + chunk(far - step).astype(f32)).astype(bf16)
    if step < near:
        behind = (behind.astype(f32) + chunk(step - near).astype(f32)).astype(bf16)
    return ahead, behind


def ring_step(whole, axis, core, state, step, *others):
    moved = None if step == 0 else ring_send(state, step)
    if others:
        moved = lax.optimization_barrier(moved + others)[:2]
    return ring_add(whole, axis, core, moved, step)


def tp_permute(values, mask):
    size = lax.axis_size("tp")
    return lax.ppermute(values, "tp", [(i, i ^ mask) for i in range(size)])


def pick_half(values, which):
    width = values.shape[-1] // 2
    return jnp.where(which == 0, values[..., :width], values[..., width:])


def join_halves(own, other, which):
    return jnp.where(
        which == 0,
        jnp.concatenate([own, other], axis=-1),
        jnp.concatenate([other, own], axis=-1),
    )


def tp_start(partial, which):
    narrow = partial.astype(jnp.bfloat16)
    moved = tp_permute(pick_half(narrow, 1 - which), 1)
    half = pick_half(partial, which) + moved.astype(jnp.float32)
    return half.astype(jnp.bfloat16)


def tp_cross(half, *others):
    moved = after(tp_permute(half, 2), *others)
    return (half.astype(jnp.float32) + moved.astype(jnp.float32)).astype(jnp.bfloat16)


def tp_join(half, which, *others):
    return join_halves(half, after(tp_permute(half, 1), *others), which).astype(jnp.float32)


def to_owners(rows, share):
    groups = rows.reshape(-1, share, rows.shape[-1])
    later = jnp.concatenate([groups[1:], jnp.zeros_like(groups[:1])], axis=0)
    return jnp.concatenate([groups, later], axis=1)


def from_owners(slots, share):
    later = jnp.concatenate([jnp.zeros_like(slots[:1, share:]), slots[:-1, share:]], axis=0)
    return (slots[:, :share] + later).reshape(-1, slots.shape[-1])


def times(left, right, left_axis, right_axis):
    return lax.dot_general(
        left,
        right,
        (((left_axis,), (right_axis,)), ((), ())),
        preferred_element_type=jnp.float32,
    )


def head_lanes(lanes, part):
    return lax.broadcasted_iota(jnp.int32, (1, lanes), 1) // HEAD_DIM == part


def forward_kernel(qkv_ref, allowed_ref, probs_ref, mixed_ref):
    width = mixed_ref.shape[1]
    lanes, each = 2 * HEAD_DIM, 2
    allowed = allowed_ref[...] != 0
    for block in range(width // lanes):
        queries, keys, values = (
            qkv_ref[:, c * width + block * lanes : c * width + (block + 1) * lanes]
            for c in range(3)
        )
        mixed = None
        for part in range(each):
            mine = head_lanes(lanes, part)
            raw = times(jnp.where(mine, queries, jnp.zeros_like(queries)), keys, 1, 1)
            logits = jnp.where(allowed, raw * HEAD_DIM ** (-0.5), -1e30)
            powered = jnp.exp(logits - jnp.max(logits, axis=-1, keepdims=True))
            probs = powered / jnp.sum(powered, axis=-1, keepdims=True)
            probs_ref[block * each + part] = probs
            product = times(probs.astype(jnp.bfloat16), values, 1, 0)
            mixed = product if part == 0 else jnp.where(mine, product, mixed)
        mixed_ref[:, block * lanes : (block + 1) * lanes] = mixed.astype(jnp.bfloat16)


def backward_kernel(qkv_ref, probs_ref, grad_ref, out_ref):
    width = grad_ref.shape[1]
    lanes, each = 2 * HEAD_DIM, 2
    for block in range(width // lanes):
        queries, keys, values = (
            qkv_ref[:, c * width + block * lanes : c * width + (block + 1) * lanes]
            for c in range(3)
        )
        grads = grad_ref[:, block * lanes : (block + 1) * lanes]
        totals = None
        for part in range(each):
            mine = head_lanes(lanes, part)
            probs = probs_ref[block * each + part]
            grad_probs = times(jnp.where(mine, grads, jnp.zeros_like(grads)), values, 1, 1)
            inner_sum = jnp.sum(probs * grad_probs, axis=-1, keepdims=True)
            grad_raw = probs * (grad_probs - inner_sum) * HEAD_DIM ** (-0.5)
            grad_raw = grad_raw.astype(jnp.bfloat16)
            products = (
                times(grad_raw, keys, 1, 0),
                times(grad_raw, queries, 0, 0),
                times(probs.astype(jnp.bfloat16), grads, 0, 0),
            )
            if part == 0:
                totals = products
            else:
                totals = tuple(jnp.where(mine, new, old) for new, old in zip(products, totals))
        for c in range(3):
            first = c * width + block * lanes
            out_ref[:, first : first + lanes] = totals[c].astype(jnp.bfloat16)


def kernel_cost(rows, width, count):
    return pl.CostEstimate(
        flops=2 * count * rows * rows * width,
        bytes_accessed=4 * rows * rows * width // HEAD_DIM + 8 * rows * width,
        transcendentals=rows * rows * width // HEAD_DIM,
    )


def attend(qkv, allowed):
    rows, width = qkv.shape[0], qkv.shape[1] // 3
    return pl.pallas_call(
        forward_kernel,
        out_shape=(
            jax.ShapeDtypeStruct((width // HEAD_DIM, rows, rows), jnp.float32),
            jax.ShapeDtypeStruct((rows, width), jnp.bfloat16),
        ),
        cost_estimate=kernel_cost(rows, width, 2),
    )(qkv, allowed)


def attend_back(qkv, probs, grads):
    rows, width = grads.shape
    return pl.pallas_call(
        backward_kernel,
        out_shape=jax.ShapeDtypeStruct(qkv.shape, jnp.bfloat16),
        cost_estimate=kernel_cost(rows, width, 5),
    )(qkv, probs, grads)


def on_device_whole(
    tokens,
    seg_ids,
    routed_index,
    gain_attn,
    w_qkv,
    w_out,
    gain_mlp,
    w_up,
    w_down,
    w_router,
    out_grad,
):
    f32, bf16 = jnp.float32, jnp.bfloat16
    seq_count, group_len, model_width = tokens.shape
    routed_len = routed_index.shape[1]
    dev_count = lax.axis_size("seq")
    dev_index = lax.axis_index("seq")
    core = lax.axis_index("tp") % 2
    side = lax.axis_index("tp") // 2
    share = routed_len // dev_count
    half_width = model_width // 2
    quarter_width = half_width // 2

    padded_index = jnp.concatenate(
        [routed_index, jnp.full((seq_count, share), -1, jnp.int32)], axis=1
    )
    slots = lax.dynamic_slice(padded_index, (0, dev_index * share), (seq_count, 2 * share))
    offsets = jnp.arange(group_len, dtype=jnp.int32)
    table = ((slots - dev_index * group_len)[:, :, None] == offsets).astype(bf16)

    index_row = lax.dynamic_index_in_dim(routed_index, dev_index, 0, False)
    seg_row = lax.dynamic_index_in_dim(seg_ids, dev_index, 0, False)
    seg_routed = sum(
        (index_row >= jnp.sum((seg_row < t).astype(jnp.int32))).astype(jnp.int32)
        for t in range(1, 4)
    )
    def pick(source, first, width):
        own = lax.dynamic_slice_in_dim(source, first, width, 2)
        return compact(table, own).astype(bf16)

    def exchange(own):
        return lax.all_to_all(own, "seq", 0, 0, tiled=True)

    def settle(slots):
        own = from_owners(slots, share)
        if own.shape[1] < half_width:
            own = join_halves(own, tp_permute(own, 2), side)
        return join_halves(own, tp_permute(own, 1), core)

    slots, seg_routed, picked_grads, weights = lax.optimization_barrier(
        (
            exchange(pick(tokens, core * half_width, half_width)),
            seg_routed,
            pick(out_grad, core * half_width + side * quarter_width, quarter_width),
            w_qkv.reshape(model_width, -1),
        )
    )
    routed_rows = settle(slots)

    ranks = jnp.arange(routed_len, dtype=jnp.int32)
    allowed = jnp.logical_and(
        ranks[None, :] <= ranks[:, None], seg_routed[None, :] == seg_routed[:, None]
    )

    rows = routed_rows.astype(f32)
    gain_first = gain_attn.astype(f32)
    gain_second = gain_mlp.astype(f32)
    router = w_router.astype(f32)
    gating = jax.nn.sigmoid(jnp.sum(rows * router, axis=-1, keepdims=True))
    factor_first = lax.rsqrt(jnp.mean(rows * rows, axis=-1, keepdims=True) + 1e-05)
    attn_input = after((rows * factor_first * gain_first).astype(bf16))
    qkv = jnp.dot(attn_input, weights, preferred_element_type=f32).astype(bf16)
    probs, mixed = attend(qkv, allowed.astype(jnp.int32))
    mixed, grad_slots = lax.optimization_barrier((mixed, exchange(picked_grads)))
    attn_half = tp_start(jnp.dot(mixed, w_out, preferred_element_type=f32), core)
    grad_rows = settle(grad_slots).astype(f32)
    attn_half = tp_cross(attn_half)
    attn_out = tp_join(attn_half, core)

    residual = rows + attn_out
    factor_second = lax.rsqrt(jnp.mean(residual * residual, axis=-1, keepdims=True) + 1e-05)
    mlp_input = (residual * factor_second * gain_second).astype(bf16)
    scaled_grad = gating * grad_rows
    grad_mlp = scaled_grad.astype(bf16)
    pre_act = jnp.dot(mlp_input, w_up, preferred_element_type=f32)
    hidden, gelu_pull = jax.vjp(gelu_tanh, pre_act)
    hidden = hidden.astype(bf16)
    grad_hidden = lax.dot_general(
        grad_mlp, w_down, (((1,), (1,)), ((), ())), preferred_element_type=f32
    )
    grad_pre = gelu_pull(grad_hidden)[0].astype(bf16)
    pull_part = lax.dot_general(
        grad_pre, w_up, (((1,), (1,)), ((), ())), preferred_element_type=f32
    )
    pull_half = tp_start(pull_part, core)
    mlp_half = tp_start(
        jnp.dot(after(hidden, pull_half), w_down, preferred_element_type=f32), core
    )

    def outer(left, right):
        product = lax.dot_general(
            left, right, (((0,), (0,)), ((), ())), preferred_element_type=f32
        )
        return product.astype(bf16)

    mlp_pairs = lax.dot_general(
        jnp.stack([mlp_input, grad_mlp]),
        jnp.stack([grad_pre, hidden]),
        (((1,), (1,)), ((0,), (0,))),
        preferred_element_type=f32,
    ).astype(bf16)

    def mlp_ring(total, step, *others):
        return ring_step(mlp_pairs, 1, core, total, step, *others)

    mlp_ring_0 = mlp_ring(None, 0)
    mlp_ring_1 = mlp_ring(mlp_ring_0, 1)
    pull_half, mlp_half = lax.optimization_barrier(
        (tp_cross(pull_half, mlp_half), mlp_half)
    )
    quarter = pick_half(attn_half, side).astype(f32) + pick_half(mlp_half, side).astype(f32)
    branch_part = quarter + tp_permute(pick_half(mlp_half, 1 - side), 2).astype(f32)
    grad_mlp_input = tp_join(pull_half, core, *mlp_ring_1)

    weighted = grad_mlp_input * gain_second
    grad_residual = factor_second * weighted - residual * factor_second**3 * jnp.mean(
        residual * weighted, axis=-1, keepdims=True
    )
    grad_gain_mlp = jnp.sum(grad_mlp_input * residual * factor_second, axis=0)
    grad_attn = (grad_residual + scaled_grad).astype(bf16)
    grad_mixed = lax.dot_general(
        grad_attn, w_out, (((1,), (1,)), ((), ())), preferred_element_type=f32
    ).astype(bf16)
    grad_parts = attend_back(qkv, probs, grad_mixed)
    mlp_ring_2 = mlp_ring(mlp_ring_1, 2)
    grad_parts, branch_part = lax.optimization_barrier((grad_parts, branch_part))
    update = (gating * branch_part).astype(bf16)
    score = jnp.sum(pick_half(pick_half(grad_rows, core), side) * branch_part, axis=-1)
    score = score + tp_permute(score, 1)
    score = score + tp_permute(score, 2)
    down_part = lax.dot_general(
        grad_parts, weights, (((1,), (1,)), ((), ())), preferred_element_type=f32
    )
    input_half = tp_start(down_part, core)

    attn_pairs = jnp.concatenate(
        [outer(attn_input, grad_parts), outer(grad_attn, mixed)], axis=1
    )

    def attn_ring(total, step, *others):
        return ring_step(attn_pairs, 0, core, total, step, *others)

    attn_ring_0 = attn_ring(None, 0)
    attn_sent = ring_send(attn_ring_0, 1)

    input_half, score = lax.optimization_barrier((tp_cross(input_half, *mlp_ring_2, *attn_ring_0), score))
    grad_score = gating * (1.0 - gating) * score[:, None]
    grad_attn_input = tp_join(input_half, core)
    weighted = grad_attn_input * gain_first
    grad_norm = factor_first * weighted - rows * factor_first**3 * jnp.mean(
        rows * weighted, axis=-1, keepdims=True
    )
    grad_gain_attn = jnp.sum(grad_attn_input * rows * factor_first, axis=0)
    grad_router = jnp.sum(grad_score * rows, axis=0)
    grad_routed_in = (grad_residual + grad_norm + grad_score * router).astype(bf16)

    small = jnp.stack([grad_gain_attn, grad_gain_mlp, grad_router]).astype(bf16)
    small = small.reshape(3, dev_count, -1).transpose(1, 0, 2)
    small = jnp.pad(small, ((0, 0), (0, 13), (0, half_width - small.shape[2])))
    grads_part = pick_half(pick_half(grad_routed_in, core), side)
    pieces = to_owners(jnp.concatenate([update, grads_part], axis=1), share)
    sent = jnp.concatenate([pieces, small], axis=1)
    sent, *attn_sent = lax.optimization_barrier((sent,) + attn_sent)
    got = lax.all_to_all(sent, "seq", 0, 0, tiled=True)
    mlp_total = mlp_ring(mlp_ring_2, 3, sent)
    attn_total = ring_add(attn_pairs, 0, core, attn_sent, 1)
    for step in range(4, dev_count // 2 + 1):
        mlp_total = mlp_ring(mlp_total, step)
    for step in range(2, dev_count // 2 + 1):
        if step == 2:
            attn_total, got = lax.optimization_barrier((attn_total, got))
        attn_total = attn_ring(attn_total, step)
    grad_up, grad_down = mlp_total[0], mlp_total[1].T
    split = 3 * mixed.shape[1]
    grad_qkv = attn_total[:, :split].reshape(-1, 3, mixed.shape[1])
    grad_out = attn_total[:, split:].T

    small = jnp.sum(got[:, 2 * share : 2 * share + 3, : model_width // dev_count].astype(f32), axis=0)
    width = half_width // 2

    def gather(part):
        part = join_halves(part, tp_permute(part, 2), side)
        return join_halves(part, tp_permute(part, 1), core)

    block_rows = gather(got[:, : 2 * share, :width])
    grad_slots = gather(got[:, : 2 * share, width:])
    block_out = (tokens.astype(f32) + spread(table, block_rows)).astype(bf16)
    grad_tokens = out_grad.astype(f32) + spread(table, grad_slots)
    return (
        block_out,
        grad_tokens,
        small[0],
        grad_qkv,
        grad_out,
        small[1],
        grad_up,
        grad_down,
        small[2],
    )


def solution(mesh):
    def on_device(*arrays):
        seq_count, routed_len = arrays[2].shape
        dev_count = mesh.shape["seq"]
        whole = seq_count == dev_count and mesh.shape["tp"] == 4 and dev_count % 2 == 0
        body = on_device_whole if whole else on_device_split
        return body(*arrays)

    return jax.shard_map(
        on_device,
        mesh=mesh,
        in_specs=(
            P(None, "seq", None),
            P(),
            P(),
            P(),
            P(None, None, "tp"),
            P("tp", None),
            P(),
            P(None, "tp"),
            P("tp", None),
            P(),
            P(None, "seq", None),
        ),
        out_specs=(
            P(None, "seq", None),
            P(None, "seq", None),
            P("seq"),
            P("seq", None, "tp"),
            P("tp", "seq"),
            P("seq"),
            P("seq", "tp"),
            P("tp", "seq"),
            P("seq"),
        ),
        check_vma=False,
    )
```
